32 devices in a mesh: fsdp: 32 (over z, y, x, core).
Axes of the slice: x: 2, y: 2, z: 4, core: 2. Of those that a mesh axis runs over, the one named last changes fastest.
Arguments:
- images: bfloat16 [2, 64, 197, 384], P(None, 'fsdp'), may hold values from -6 to 6
- counts: int32 [2, 32], P(None, 'fsdp'), may hold values from 1 to 2, as said below
- out_grad: bfloat16 [2, 64, 197, 384], P(None, 'fsdp'), may hold values from -6 to 6
- qkv_weight: bfloat16 [442368], P('fsdp'), may hold values from -0.3125 to 0.3125
- out_weight: bfloat16 [147456], P('fsdp'), may hold values from -1.75 to 1.75
- fc1_weight: bfloat16 [589824], P('fsdp'), may hold values from -0.3125 to 0.3125
- fc2_weight: bfloat16 [589824], P('fsdp'), may hold values from -0.15625 to 0.15625
- norm_gains: bfloat16 [768], P('fsdp'), may hold values from 0.5 to 1.5
- biases: bfloat16 [3840], P('fsdp'), may hold values from -3 to 3
Outputs:
- block_out: float32 [2, 64, 197, 384], P(None, 'fsdp')
- input_grad: float32 [2, 64, 197, 384], P(None, 'fsdp')
- qkv_grad: float32 [442368], P('fsdp')
- out_grad_weight: float32 [147456], P('fsdp')
- fc1_grad: float32 [589824], P('fsdp')
- fc2_grad: float32 [589824], P('fsdp')
- gain_grad: float32 [768], P('fsdp')
- bias_grad: float32 [3840], P('fsdp')
The draws below stay inside these ranges and needn't reach their ends.
Inputs may be any that keep to these rules, and one draw needn't show every extreme that they name: Device d holds counts[m, d] live images of micro-batch m in its first slots; its other slots of the 2 are empty. In every micro-batch some device holds 2 and some holds 1.
All inputs are finite; a program needn't handle non-finite values.
Results may differ from the reference program's by a relative error of at most 0.0098.
Values may be sent and summed in bfloat16 or wider, within the bound.
No kernel may reach another device: no remote copies, remote signals or barrier semaphores. Data moves between devices by JAX's collectives and lax.ppermute only.
A program may use at most 128 MiB of HBM per device.

```python
import jax
import jax.numpy as jnp
from jax import lax

D = 384
H = 6
FF = 1536
HD = 64
S = 197
MB = 2
CAP = 2
SLOTS = 64
N_FSDP = 32


def draw_counts(key, part):
    key_base = jax.random.fold_in(key, 11)
    key_high = jax.random.fold_in(key, 12)
    key_less = jax.random.fold_in(key, 13)
    drawn = jax.random.randint(key_base, (MB, N_FSDP), CAP - 1, CAP + 1)
    high_slot = jax.random.randint(key_high, (MB, 1), 0, N_FSDP)
    less_slot = (high_slot + 1 + jax.random.randint(key_less, (MB, 1), 0, N_FSDP - 1)) % N_FSDP
    columns = jnp.arange(N_FSDP, dtype=jnp.int32)[None, :]
    drawn = jnp.where(columns == high_slot, CAP, drawn)
    drawn = jnp.where(columns == less_slot, CAP - 1, drawn)
    return drawn.astype(jnp.int32)


def block_scale(rng, dims, split, least, largest):
    factor_of, own = 1.0, jax.random.fold_in(rng, 6)
    for dim, blocks in split:
        heights = jnp.exp(jax.random.uniform(jax.random.fold_in(own, dim), (blocks,), jnp.float32, least / len(split), largest / len(split)))
        factor_of = factor_of * jnp.repeat(heights, dims[dim] // blocks).reshape([-1 if axis == dim else 1 for axis in range(len(dims))])
    return factor_of


def normal_values(own_key, extent, width, reach, split=(), kind=jnp.bfloat16):
    factor_of = block_scale(own_key, extent, split, -0.22, 0.18) if split else 1.0
    entries = jax.random.normal(own_key, extent, jnp.float32) * width * factor_of
    return jnp.minimum(jnp.maximum(entries, -reach), reach).astype(kind)


def setup_inputs(seed: int = 0) -> dict:
    streams_of = jax.random.split(jax.random.key(seed), 10)
    images = normal_values(streams_of[0], (MB, SLOTS, S, D), 1.0, 6.0, ((1, 32),))
    counts = draw_counts(jax.random.fold_in(streams_of[9], 71), 0)
    out_grad = normal_values(streams_of[2], (MB, SLOTS, S, D), 1.0, 6.0, ((1, 32),))
    qkv_weight = normal_values(streams_of[3], (3 * D * D,), D ** -0.5, 0.3125, ((0, 32),))
    out_weight = normal_values(streams_of[4], (D * D,), (D // 32) ** -0.5, 1.75, ((0, 32),))
    fc1_weight = normal_values(streams_of[5], (D * FF,), D ** -0.5, 0.3125, ((0, 32),))
    fc2_weight = normal_values(streams_of[6], (FF * D,), FF ** -0.5, 0.15625, ((0, 32),))
    norm_gains = jnp.clip(1.0 + 0.1 * jax.random.normal(streams_of[7], (2 * D,), jnp.float32), 0.5, 1.5).astype(jnp.bfloat16)
    biases = normal_values(streams_of[8], (6 * D + FF,), 0.5, 3.0, ((0, 32),))
    return dict(images=images, counts=counts, out_grad=out_grad, qkv_weight=qkv_weight, out_weight=out_weight, fc1_weight=fc1_weight, fc2_weight=fc2_weight, norm_gains=norm_gains, biases=biases)


@jax.custom_vjp
def low(v):
    return lax.optimization_barrier(v.astype(jnp.bfloat16)).astype(jnp.float32)

@jax.custom_vjp
def low_back(v):
    return v

def low_keep(v):
    return (low(v), None)

def low_pass(kept, grad):
    return (grad,)

def back_keep(v):
    return (v, None)

def back_low(kept, grad):
    return (low(grad),)
low.defvjp(low_keep, low_pass)
low_back.defvjp(back_keep, back_low)
highest = lax.Precision.HIGHEST
eps_norm = 1e-06

def norm_rows(rows_in, gain_vec, shift_vec):
    row_mean = lax.optimization_barrier(jnp.mean(rows_in, axis=-1, keepdims=True))
    centred = rows_in - row_mean
    variance = lax.optimization_barrier(jnp.mean(centred * centred, axis=-1, keepdims=True))
    return centred * lax.rsqrt(variance + eps_norm) * gain_vec + shift_vec

def block_forward(params, image_block, live_block):
    qkv_w, out_w, fc1_w, fc2_w, gain_all, bias_all = params
    count_img = image_block.shape[0]
    row_count = count_img * S
    shape_heads = (count_img, S, H, HD)
    rows_in = image_block.reshape(row_count, D)
    normed = low(norm_rows(rows_in, gain_all[:D], bias_all[:D]))
    mixed = jnp.dot(normed, qkv_w, precision=highest)
    query_rows = low(low_back(mixed[:, :D] + bias_all[4 * D:5 * D]))
    key_rows = low(low_back(mixed[:, D:2 * D]))
    value_rows = low(low_back(mixed[:, 2 * D:] + bias_all[5 * D:6 * D]))
    scores = jnp.einsum('bqhd,bkhd->bhqk', query_rows.reshape(shape_heads), key_rows.reshape(shape_heads), precision=highest) * (1.0 / HD ** 0.5)
    scores = low_back(scores)
    weights = low(jax.nn.softmax(scores, axis=-1))
    attended = jnp.einsum('bhqk,bkhd->bqhd', weights, value_rows.reshape(shape_heads), precision=highest)
    attended = low(low_back(attended.reshape(row_count, D)))
    branch = low_back(jnp.dot(attended, out_w, precision=highest) + bias_all[2 * D:3 * D])
    residual = rows_in + branch
    normed_two = low(norm_rows(residual, gain_all[D:], bias_all[D:2 * D]))
    hidden_in = low_back(jnp.dot(normed_two, fc1_w, precision=highest) + bias_all[6 * D:])
    active = low(jax.nn.gelu(hidden_in, approximate=False))
    branch_two = low_back(jnp.dot(active, fc2_w, precision=highest) + bias_all[3 * D:4 * D])
    result_rows = (residual + branch_two).reshape(image_block.shape)
    return result_rows * live_block[:, None, None]

def reference(images, counts, out_grad, qkv_weight, out_weight, fc1_weight, fc2_weight, norm_gains, biases):
    params = (qkv_weight.astype(jnp.float32).reshape(D, 3 * D), out_weight.astype(jnp.float32).reshape(D, D), fc1_weight.astype(jnp.float32).reshape(D, FF), fc2_weight.astype(jnp.float32).reshape(FF, D), norm_gains.astype(jnp.float32), biases.astype(jnp.float32))
    slot_total = images.shape[1]
    local_slot = jnp.arange(slot_total, dtype=jnp.int32) % CAP
    live = (local_slot[None, :] < jnp.repeat(counts, CAP, axis=1)).astype(jnp.float32)
    group = 8 * CAP
    grouped = images.astype(jnp.float32).reshape(-1, group, S, D)
    live_groups = live.reshape(-1, group)

    def forward(params_in, grouped_in):
        block_step = jax.checkpoint(lambda image_block, live_block: block_forward(params_in, image_block, live_block))
        return lax.map(lambda item: block_step(item[0], item[1]), (grouped_in, live_groups))
    outputs, pullback = jax.vjp(forward, params, grouped)
    param_grads, input_grads = pullback(out_grad.astype(jnp.float32).reshape(grouped.shape))
    block_out = outputs.reshape(images.shape)
    input_grad = input_grads.reshape(images.shape)
    return (block_out, input_grad, param_grads[0].reshape(-1), param_grads[1].reshape(-1), param_grads[2].reshape(-1), param_grads[3].reshape(-1), param_grads[4], param_grads[5])
```

```python
import functools
import math

import jax
import jax.numpy as jnp
from jax import lax
from jax.experimental import pallas as pl
from jax.experimental.pallas import tpu as pltpu
from jax.sharding import PartitionSpec as P

D = 384
H = 6
FF = 1536
HD = 64
S = 197
SP = 208
SQ = 256
EPS = 1e-06
f32 = jnp.float32
bf16 = jnp.bfloat16
G1, G2, B1, B2, BO, BF2, BQ, BV, BF1 = 0, 384, 768, 1152, 1536, 1920, 2304, 2688, 3072
NV = 4608
VMEM_LIMIT = 60 * 1024 * 1024


def params(**kw):
    return pltpu.CompilerParams(vmem_limit_bytes=VMEM_LIMIT, **kw)


def full(shape):
    return pl.BlockSpec(shape, lambda *_: (0,) * len(shape))


def any_spec():
    return pl.BlockSpec(memory_space=pl.ANY)


def nn(a, b):
    return jnp.dot(a, b, preferred_element_type=f32)


def nt(a, b):
    return lax.dot_general(a, b, (((1,), (1,)), ((), ())), preferred_element_type=f32)


def tr(a):
    return a.astype(f32).T.astype(a.dtype)


def norm_stats(rows):
    mean = jnp.mean(rows, axis=-1, keepdims=True)
    cen = rows - mean
    var = jnp.mean(cen * cen, axis=-1, keepdims=True)
    inv = lax.rsqrt(var + EPS)
    return cen * inv, inv


def pad_rows(ref_val):
    return jnp.concatenate([ref_val, jnp.zeros((SP - S, ref_val.shape[1]), ref_val.dtype)], axis=0)


def head_masks():
    lane = lax.broadcasted_iota(jnp.int32, (SP, 128), 1)
    return lane < HD


def pick(block, first, head):
    zero = jnp.zeros_like(block)
    return jnp.where(first, block, zero) if head == 0 else jnp.where(first, zero, block)


def attn_fwd_body(x_ref, w, vec, a1_ref, qkv_ref, o_ref, lse_ref):
    rows = pad_rows(x_ref[0].astype(f32))
    n1, _ = norm_stats(rows)
    a1 = (n1 * vec[:, G1 : G1 + D] + vec[:, B1 : B1 + D]).astype(bf16)
    a1_ref[0] = a1
    mixed = nn(a1, w)
    q = (mixed[:, :D] + vec[:, BQ : BQ + D]).astype(bf16)
    k = mixed[:, D : 2 * D].astype(bf16)
    v = (mixed[:, 2 * D :] + vec[:, BV : BV + D]).astype(bf16)
    qkv_ref[0, :, :D] = q
    qkv_ref[0, :, D : 2 * D] = k
    qkv_ref[0, :, 2 * D :] = v
    first = head_masks()
    key_ok = lax.broadcasted_iota(jnp.int32, (SP, SQ), 0) < S
    for j in range(H // 2):
        cols = slice(128 * j, 128 * j + 128)
        q2t = jnp.concatenate([tr(q[:, cols]), jnp.zeros((128, SQ - SP), bf16)], axis=1)
        v2t = tr(v[:, cols])
        outs = []
        for h in range(2):
            z = nn(pick(k[:, cols], first, h), q2t) * 0.125
            z = jnp.where(key_ok, z, -1e30)
            peak = jnp.max(z, axis=0, keepdims=True)
            e = jnp.exp(z - peak)
            total = jnp.sum(e, axis=0, keepdims=True)
            pb = (e * (1.0 / total)).astype(bf16)
            lse_ref[0, pl.ds(2 * j + h, 1), :] = peak + jnp.log(total)
            outs.append(nn(v2t[HD * h : HD * h + HD, :], pb))
        o_ref[0, :, cols] = jnp.concatenate(outs, axis=0).T[:SP].astype(bf16)


def k1_kernel(x_ref, w_ref, vec_ref, a1_ref, qkv_ref, o_ref, lse_ref):
    attn_fwd_body(x_ref, w_ref[...], vec_ref[...], a1_ref, qkv_ref, o_ref, lse_ref)


def k1(x, w, vec):
    n = x.shape[0]
    blk = lambda r, c: pl.BlockSpec((1, r, c), lambda i: (i, 0, 0))
    return pl.pallas_call(
        k1_kernel,
        name="k1",
        grid=(n,),
        in_specs=[blk(S, D), full((D, 3 * D)), full((1, NV))],
        out_specs=[blk(SP, D), blk(SP, 3 * D), blk(SP, D), blk(8, SQ)],
        out_shape=[
            jax.ShapeDtypeStruct((n, SP, D), bf16),
            jax.ShapeDtypeStruct((n, SP, 3 * D), bf16),
            jax.ShapeDtypeStruct((n, SP, D), bf16),
            jax.ShapeDtypeStruct((n, 8, SQ), f32),
        ],
        compiler_params=params(),
    )(x, w, vec)


CH = 768


def gelu_parts(u):
    cum = 0.5 * (1.0 + lax.erf(u * (1.0 / math.sqrt(2.0))))
    den = jnp.exp(-0.5 * u * u) * (1.0 / math.sqrt(2.0 * math.pi))
    return u * cum, cum + u * den


def k2_kernel(live_ref, x_ref, g_ref, o_ref, oall_ref, wo_ref, w1_ref, w2_ref, vec_ref,
              out_ref, dr_ref, go_ref, g1_ref, g2_ref, sums_ref, a2_s, du_s, gl_s, eb_s, drb_s):
    i = pl.program_id(0)
    n = pl.num_programs(0)
    vec = vec_ref[...]
    live = live_ref[i]
    rows = pl.ds(i * SP, SP)

    @pl.when(i == 0)
    def _():
        sums_ref[...] = jnp.zeros_like(sums_ref)

    res = pad_rows(x_ref[0].astype(f32)) + nn(o_ref[0], wo_ref[...]) + vec[:, BO : BO + D]
    n2, r2 = norm_stats(res)
    a2 = (n2 * vec[:, G2 : G2 + D] + vec[:, B2 : B2 + D]).astype(bf16)
    a2_s[rows, :] = a2
    e = pad_rows(g_ref[0].astype(f32)) * live
    eb = e.astype(bf16)
    eb_s[rows, :] = eb
    acc = res + vec[:, BF2 : BF2 + D]
    dn = jnp.zeros((SP, D), f32)
    for c in range(FF // CH):
        cs = slice(CH * c, CH * c + CH)
        u = nn(a2, w1_ref[:, cs]) + vec[:, BF1 + CH * c : BF1 + CH * c + CH]
        dg = nt(eb, w2_ref[cs, :])
        gel, slope = gelu_parts(u)
        gb = gel.astype(bf16)
        du = (dg * slope).astype(bf16)
        gl_s[rows, cs] = gb
        du_s[rows, cs] = du
        acc = acc + nn(gb, w2_ref[cs, :])
        dn = dn + nt(du, w1_ref[:, cs])
    out_ref[0] = (acc * live)[:S]
    t = dn * vec[:, G2 : G2 + D]
    dr = e + r2 * (
        t - jnp.mean(t, axis=-1, keepdims=True) - n2 * jnp.mean(t * n2, axis=-1, keepdims=True)
    )
    dr_ref[0] = dr
    drb_s[rows, :] = dr.astype(bf16)
    sums_ref[0:1, G2 : G2 + D] += jnp.sum(dn * n2, axis=0, keepdims=True)
    sums_ref[0:1, B2 : B2 + D] += jnp.sum(dn, axis=0, keepdims=True)

    @pl.when(i == n - 1)
    def _():
        ones = jnp.ones((8, a2_s.shape[0]), bf16)
        eball = eb_s[...]
        drball = drb_s[...]
        g1_ref[...] = nn(tr(a2_s[...]), du_s[...])
        g2_ref[...] = nn(tr(eball), gl_s[...]).T
        go_ref[...] = nn(tr(oall_ref[...].reshape(-1, D)), drball)
        sums_ref[:, BF1 : BF1 + FF] = nn(ones, du_s[...])
        sums_ref[:, BF2 : BF2 + D] = nn(ones, eball)
        sums_ref[:, BO : BO + D] = nn(ones, drball)


def k2(live, x, g, o, wo, w1, w2, vec):
    n = x.shape[0]
    blk = lambda r, c: pl.BlockSpec((1, r, c), lambda i: (i, 0, 0))
    return pl.pallas_call(
        k2_kernel,
        name="k2",
        grid=(n,),
        in_specs=[pl.BlockSpec(memory_space=pltpu.SMEM), blk(S, D), blk(S, D), blk(SP, D), full((n, SP, D)),
                  full((D, D)), full((D, FF)), full((FF, D)), full((1, NV))],
        out_specs=[blk(S, D), blk(SP, D), full((D, D)), full((D, FF)), full((FF, D)), full((8, NV))],
        out_shape=[
            jax.ShapeDtypeStruct((n, S, D), f32),
            jax.ShapeDtypeStruct((n, SP, D), f32),
            jax.ShapeDtypeStruct((D, D), f32),
            jax.ShapeDtypeStruct((D, FF), f32),
            jax.ShapeDtypeStruct((FF, D), f32),
            jax.ShapeDtypeStruct((8, NV), f32),
        ],
        scratch_shapes=[
            pltpu.VMEM((n * SP, D), bf16),
            pltpu.VMEM((n * SP, FF), bf16),
            pltpu.VMEM((n * SP, FF), bf16),
            pltpu.VMEM((n * SP, D), bf16),
            pltpu.VMEM((n * SP, D), bf16),
        ],
        compiler_params=params(),
    )(live, x, g, o, o, wo, w1, w2, vec)


def k3_kernel(x_ref, qkv_ref, lse_ref, dr_ref, a1_ref, w_ref, wo_ref, vec_ref,
              dx_ref, gq_ref, sums_ref, dp_s):
    i = pl.program_id(0)
    n = pl.num_programs(0)
    vec = vec_ref[...]
    rows = pl.ds(i * SP, SP)

    @pl.when(i == 0)
    def _():
        sums_ref[...] = jnp.zeros_like(sums_ref)

    dr = dr_ref[0]
    do = nt(dr.astype(bf16), wo_ref[...]).astype(bf16)
    first = head_masks()
    key_ok = lax.broadcasted_iota(jnp.int32, (SP, SQ), 0) < S
    lanes0 = jnp.zeros((128, SQ - SP), bf16)
    rows0 = jnp.zeros((SQ - SP, 128), bf16)
    for j in range(H // 2):
        q2 = qkv_ref[0, :, 128 * j : 128 * j + 128]
        k2_ = qkv_ref[0, :, D + 128 * j : D + 128 * j + 128]
        v2 = qkv_ref[0, :, 2 * D + 128 * j : 2 * D + 128 * j + 128]
        do2 = do[:, 128 * j : 128 * j + 128]
        q2t = jnp.concatenate([tr(q2), lanes0], axis=1)
        do2t = jnp.concatenate([tr(do2), lanes0], axis=1)
        k2t = tr(k2_)
        dqs = []
        dk = jnp.zeros((SP, 128), f32)
        dv = jnp.zeros((SP, 128), f32)
        for h in range(2):
            z = nn(pick(k2_, first, h), q2t) * 0.125
            z = jnp.where(key_ok, z, -1e30)
            p = jnp.exp(z - lse_ref[0, pl.ds(2 * j + h, 1), :])
            dpr = nn(pick(v2, first, h), do2t)
            dot_row = jnp.sum(p * dpr, axis=0, keepdims=True)
            dz = (p * (dpr - dot_row)).astype(bf16)
            pb = p.astype(bf16)
            dv = dv + nn(pb, jnp.concatenate([pick(do2, first, h), rows0], axis=0))
            dk = dk + nn(dz, jnp.concatenate([pick(q2, first, h), rows0], axis=0))
            dqs.append(nn(k2t[HD * h : HD * h + HD, :], dz))
        dp_s[rows, 128 * j : 128 * j + 128] = (jnp.concatenate(dqs, axis=0).T[:SP] * 0.125).astype(bf16)
        dp_s[rows, D + 128 * j : D + 128 * j + 128] = (dk * 0.125).astype(bf16)
        dp_s[rows, 2 * D + 128 * j : 2 * D + 128 * j + 128] = dv.astype(bf16)
    dn = nt(dp_s[rows, :], w_ref[...])
    n1, r1 = norm_stats(pad_rows(x_ref[0].astype(f32)))
    t = dn * vec[:, G1 : G1 + D]
    dx = dr + r1 * (
        t - jnp.mean(t, axis=-1, keepdims=True) - n1 * jnp.mean(t * n1, axis=-1, keepdims=True)
    )
    dx_ref[0] = dx[:S]
    sums_ref[0:1, G1 : G1 + D] += jnp.sum(dn * n1, axis=0, keepdims=True)
    sums_ref[0:1, B1 : B1 + D] += jnp.sum(dn, axis=0, keepdims=True)

    @pl.when(i == n - 1)
    def _():
        dpall = dp_s[...]
        gq_ref[...] = nn(tr(a1_ref[...].reshape(-1, D)), dpall)
        bsum = nn(jnp.ones((8, dpall.shape[0]), bf16), dpall)
        sums_ref[:, BQ : BQ + D] = bsum[:, :D]
        sums_ref[:, BV : BV + D] = bsum[:, 2 * D :]


def k3(x, qkv, lse, dr, a1, w, wo, vec):
    n = x.shape[0]
    blk = lambda r, c: pl.BlockSpec((1, r, c), lambda i: (i, 0, 0))
    return pl.pallas_call(
        k3_kernel,
        name="k3",
        grid=(n,),
        in_specs=[blk(S, D), blk(SP, 3 * D), blk(8, SQ), blk(SP, D), full((n, SP, D)),
                  full((D, 3 * D)), full((D, D)), full((1, NV))],
        out_specs=[blk(S, D), full((D, 3 * D)), full((8, NV))],
        out_shape=[
            jax.ShapeDtypeStruct((n, S, D), f32),
            jax.ShapeDtypeStruct((D, 3 * D), f32),
            jax.ShapeDtypeStruct((8, NV), f32),
        ],
        scratch_shapes=[pltpu.VMEM((n * SP, 3 * D), bf16)],
        compiler_params=params(),
    )(x, qkv, lse, dr, a1, w, wo, vec)


def local(images, counts, out_grad, qkv_weight, out_weight, fc1_weight, fc2_weight, norm_gains, biases):
    ag = lambda v: lax.all_gather(v, "fsdp", axis=0, tiled=True)
    w = ag(qkv_weight).reshape(D, 3 * D)
    wo = ag(out_weight).reshape(D, D)
    w1 = ag(fc1_weight).reshape(D, FF)
    w2 = ag(fc2_weight).reshape(FF, D)
    vec = jnp.concatenate([ag(norm_gains), ag(biases)]).astype(f32)[None, :]
    mb, cap = images.shape[:2]
    x = images.reshape(mb * cap, S, D)
    g = out_grad.reshape(mb * cap, S, D)
    live = (jnp.arange(cap, dtype=jnp.int32)[None, :] < counts[:, :1]).astype(f32).reshape(-1)
    a1, qkv, o, lse = k1(x, w, vec)
    out, dr, go, g1, g2, sums2 = k2(live, x, g, o, wo, w1, w2, vec)
    dx, gq, sums3 = k3(x, qkv, lse, dr, a1, w, wo, vec)
    sums = jnp.where((jnp.arange(NV) < G2) | ((jnp.arange(NV) >= B1) & (jnp.arange(NV) < B2)) | ((jnp.arange(NV) >= BQ) & (jnp.arange(NV) < BF1)), sums3[0], sums2[0])
    rs = lambda v: lax.psum_scatter(v.reshape(-1), "fsdp", scatter_dimension=0, tiled=True)
    return (out.reshape(images.shape), dx.reshape(images.shape), rs(gq), rs(go), rs(g1), rs(g2), rs(sums[: 2 * D]), rs(sums[2 * D :]))


def solution(mesh):
    placed = (
        P(None, "fsdp", None, None),
        P(None, "fsdp"),
        P(None, "fsdp", None, None),
        P("fsdp"),
        P("fsdp"),
        P("fsdp"),
        P("fsdp"),
        P("fsdp"),
        P("fsdp"),
    )
    return jax.shard_map(
        local,
        mesh=mesh,
        in_specs=placed,
        out_specs=(placed[0], placed[2]) + (P("fsdp"),) * 6,
        check_vma=False,
    )
```

```python
import functools
import math

import jax
import jax.numpy as jnp
from jax import lax
from jax.experimental import pallas as pl
from jax.experimental.pallas import tpu as pltpu
from jax.sharding import PartitionSpec as P


D = 384
H = 6
FF = 1536
HD = 64
S = 197
SP = 208
SQ = 256
EPS = 1e-06
f32 = jnp.float32
bf16 = jnp.bfloat16
G1, G2, B1, B2, BO, BF2, BQ, BV, BF1 = 0, 384, 768, 1152, 1536, 1920, 2304, 2688, 3072
NV = 4608
VMEM_LIMIT = 60 * 1024 * 1024


def params(**kw):
    return pltpu.CompilerParams(vmem_limit_bytes=VMEM_LIMIT, **kw)


def full(shape):
    return pl.BlockSpec(shape, lambda *_: (0,) * len(shape))


def any_spec():
    return pl.BlockSpec(memory_space=pl.ANY)


def nn(a, b):
    return jnp.dot(a, b, preferred_element_type=f32)


def nt(a, b):
    return lax.dot_general(a, b, (((1,), (1,)), ((), ())), preferred_element_type=f32)


def tr(a):
    return a.astype(f32).T.astype(a.dtype)


def norm_stats(rows):
    mean = jnp.mean(rows, axis=-1, keepdims=True)
    cen = rows - mean
    var = jnp.mean(cen * cen, axis=-1, keepdims=True)
    inv = lax.rsqrt(var + EPS)
    return cen * inv, inv


def pad_rows(ref_val):
    return jnp.concatenate([ref_val, jnp.zeros((SP - S, ref_val.shape[1]), ref_val.dtype)], axis=0)


def head_masks():
    lane = lax.broadcasted_iota(jnp.int32, (SP, 128), 1)
    return lane < HD


def pick(block, first, head):
    zero = jnp.zeros_like(block)
    return jnp.where(first, block, zero) if head == 0 else jnp.where(first, zero, block)


TAIL = S // 8 * 8


def mask_tail(z):
    ok = lax.broadcasted_iota(jnp.int32, (SP - TAIL, z.shape[1]), 0) < S - TAIL
    return jnp.concatenate([z[:TAIL], jnp.where(ok, z[TAIL:], -1e30)], axis=0)


def attn_fwd_body(x_ref, w, vec, a1_ref, qkv_ref, o_ref, lse_ref, n1_ref):
    rows = pad_rows(x_ref[0].astype(f32))
    n1, _ = norm_stats(rows)
    a1 = (n1 * vec[:, G1 : G1 + D] + vec[:, B1 : B1 + D]).astype(bf16)
    a1_ref[0] = a1
    n1_ref[0] = n1.astype(bf16)
    mixed = nn(a1, w)
    q = (mixed[:, :D] + vec[:, BQ : BQ + D]).astype(bf16)
    k = mixed[:, D : 2 * D].astype(bf16)
    v = (mixed[:, 2 * D :] + vec[:, BV : BV + D]).astype(bf16)
    qkv_ref[0, :, :D] = q
    qkv_ref[0, :, D : 2 * D] = k
    qkv_ref[0, :, 2 * D :] = v
    first = head_masks()
    for j in range(H // 2):
        cols = slice(128 * j, 128 * j + 128)
        q2t = jnp.concatenate([tr(q[:, cols] * 0.125), jnp.zeros((128, SQ - SP), bf16)], axis=1)
        v2t = tr(v[:, cols])
        outs = []
        for h in range(2):
            z = mask_tail(nn(pick(k[:, cols], first, h), q2t))
            peak = jnp.max(z, axis=0, keepdims=True)
            e = jnp.exp(z - peak)
            total = jnp.sum(e, axis=0, keepdims=True)
            pb = (e * (1.0 / total)).astype(bf16)
            lse_ref[0, pl.ds(2 * j + h, 1), :] = peak + jnp.log(total)
            outs.append(nn(v2t[HD * h : HD * h + HD, :], pb))
        o_ref[0, :, cols] = jnp.concatenate(outs, axis=0).T[:SP].astype(bf16)


def cost(flops, nbytes, trans=0):
    return pl.CostEstimate(flops=int(flops), bytes_accessed=int(nbytes), transcendentals=int(trans))


def smem():
    return pl.BlockSpec(memory_space=pltpu.SMEM)


C1, C2 = 640, 1792
CF, CO = 768, 1024


def prep_kernel(core_ref, q_ref, o_ref, f1_ref, f2_ref, g_ref, b_ref, own_ref, send_ref, qs, os_, f1s, f2s):
    rows = own_ref.shape[0]
    core = core_ref[0]
    qs[...] = q_ref[...].astype(f32)
    os_[...] = o_ref[...].astype(f32)
    f1s[...] = f1_ref[...].astype(f32)
    f2s[...] = f2_ref[...].astype(f32)
    sets = []
    for s in range(2):
        parts = []
        for b in range(5):
            col = 5 * s + b
            if col < 9:
                parts.append(qs[pl.ds(col, rows, stride=9), :])
            else:
                small = jnp.zeros((rows, 128), f32)
                row = lax.broadcasted_iota(jnp.int32, (rows, 128), 0)
                gains = jnp.concatenate([g_ref[...].astype(f32), jnp.zeros((1, 128 - g_ref.shape[1]), f32)], axis=1)
                shifts = jnp.concatenate([b_ref[...].astype(f32), jnp.zeros((1, 128 - b_ref.shape[1]), f32)], axis=1)
                small = jnp.where(row == 0, gains, jnp.where(row == 1, shifts, small))
                parts.append(small)
        for b in range(6):
            parts.append(f1s[pl.ds(6 * s + b, rows, stride=12), :])
        for b in range(2):
            parts.append(os_[pl.ds(s + b, rows, stride=3), :])
        for half in range(2):
            for b in range(3):
                parts.append(f2s[pl.ds(3 * (2 * rows * s + rows * half) + b, rows, stride=3), :])
        sets.append(jnp.concatenate(parts, axis=1))
    own_ref[...] = jnp.where(core == 0, sets[0], sets[1]).astype(bf16)
    send_ref[...] = jnp.where(core == 0, sets[1], sets[0]).astype(bf16)


def prep(core, q, o, f1, f2, g, b):
    rows = q.shape[0] // 9
    shape = jax.ShapeDtypeStruct((rows, C1 + C2), bf16)
    vm = pl.BlockSpec(memory_space=pltpu.VMEM)
    return pl.pallas_call(
        prep_kernel, name="prep", in_specs=[smem()] + [vm] * 6, out_specs=[vm] * 2, out_shape=[shape] * 2,
        scratch_shapes=[pltpu.VMEM(v.shape, f32) for v in (q, o, f1, f2)],
        compiler_params=params(),
    )(core, q, o, f1, f2, g, b)


def merge_kernel(core_ref, own_ref, recv_ref, p1_ref, p2_ref):
    core = core_ref[0]
    own = own_ref[...].astype(f32)
    recv = recv_ref[...].astype(f32)
    top = jnp.where(core == 0, own, recv)
    low = jnp.where(core == 0, recv, own)
    cat = lambda a, b: jnp.concatenate([a, b], axis=0).astype(bf16)
    p1 = cat(top[:, :C1], low[:, :C1])
    for k in range(p1_ref.shape[0]):
        p1_ref[k] = p1
    p2_ref[:, :CO] = cat(top[:, C1 : C1 + CO], low[:, C1 : C1 + CO])
    for c, v in ((0, top), (1, low)):
        base = C1 + CO
        p2_ref[:, CO + D * c : CO + D * c + D] = cat(v[:, base : base + D], v[:, base + D : base + 2 * D])


def merge(core, own, recv, chips):
    rows = own.shape[0]
    vm = pl.BlockSpec(memory_space=pltpu.VMEM)
    return pl.pallas_call(
        merge_kernel, name="merge", in_specs=[smem(), vm, vm], out_specs=[vm] * 2,
        out_shape=[jax.ShapeDtypeStruct((chips, 2 * rows, C1), bf16), jax.ShapeDtypeStruct((2 * rows, C2), bf16)],
        compiler_params=params(),
    )(core, own, recv)


def k0_kernel(core_ref, own_ref, recv_ref, w_ref, vec_ref, m_s, *, n):
    core = core_ref[0]
    own = own_ref[...]
    recv = recv_ref[...]
    first = jnp.where(core == 0, own, recv)
    second = jnp.where(core == 0, recv, own)
    w_ref[:, :C1] = first
    w_ref[:, C1:] = second[:, : 3 * D - C1]
    m_s[...] = second[:, 3 * D - C1 :].astype(f32)
    per = D // n
    ng, nb = 2 * D // n, (NV - 2 * D) // n
    for d in range(n):
        vec_ref[0:1, ng * d : ng * d + ng] = m_s[per * d : per * d + 1, :ng]
        vec_ref[0:1, 2 * D + nb * d : 2 * D + nb * d + nb] = m_s[per * d + 1 : per * d + 2, :nb]


def k0(core, own, recv, n):
    vm = pl.BlockSpec(memory_space=pltpu.VMEM)
    return pl.pallas_call(
        functools.partial(k0_kernel, n=n), name="k0", in_specs=[smem(), vm, vm], out_specs=[vm, vm],
        out_shape=[jax.ShapeDtypeStruct((D, 3 * D), bf16), jax.ShapeDtypeStruct((1, NV), f32)],
        scratch_shapes=[pltpu.VMEM((D, 128), f32)],
        compiler_params=params(),
    )(core, own, recv)


def k1_kernel(x_ref, w_ref, vec_ref, *rest):
    attn_fwd_body(x_ref, w_ref[...], vec_ref[...], *rest[-5:])


def k1(x, w, vec, start, count, prev=()):
    n = x.shape[0]
    blk = lambda r, c: pl.BlockSpec((1, r, c), lambda i: (i + start, 0, 0))
    return pl.pallas_call(
        k1_kernel,
        name="k1",
        grid=(count,),
        in_specs=[blk(S, D), full((D, 3 * D)), full((1, NV))] + [any_spec()] * len(prev),
        out_specs=[blk(SP, D), blk(SP, 3 * D), blk(SP, D), blk(8, SQ), blk(SP, D)],
        out_shape=[
            jax.ShapeDtypeStruct((n, SP, D), bf16),
            jax.ShapeDtypeStruct((n, SP, 3 * D), bf16),
            jax.ShapeDtypeStruct((n, SP, D), bf16),
            jax.ShapeDtypeStruct((n, 8, SQ), f32),
            jax.ShapeDtypeStruct((n, SP, D), bf16),
        ],
        input_output_aliases={3 + k: k for k in range(len(prev))},
        cost_estimate=cost(count * 1e9, count * 1e6, count * 3e5),
        compiler_params=params(),
    )(x, w, vec, *prev)


CH = 768


def gelu_parts(u):
    cum = 0.5 * (1.0 + lax.erf(u * (1.0 / math.sqrt(2.0))))
    den = jnp.exp(-0.5 * u * u) * (1.0 / math.sqrt(2.0 * math.pi))
    return u * cum, cum + u * den


def k2_kernel(core_ref, live_ref, x_ref, g_ref, o_ref, oall_ref, owna_ref, ownb_ref, recva_ref, recvb_ref, vec_ref,
              out_ref, dr_ref, keep_ref, send_ref, wo_ref, sums_ref,
              a2_s, du_s, gl_s, eb_s, drb_s, w1_ref, w2_ref, *, pieces, cap):
    i = pl.program_id(0)
    n = pl.num_programs(0)
    core = core_ref[0]
    unit = D // pieces
    vec = vec_ref[...]
    live = (lax.rem(i, cap) < live_ref[lax.div(i, cap), 0]).astype(f32)
    rows = pl.ds(i * SP, SP)

    @pl.when(i == 0)
    def _():
        sums_ref[...] = jnp.zeros_like(sums_ref)
        own = jnp.concatenate([owna_ref[...], ownb_ref[...]], axis=1)
        recv = jnp.concatenate([recva_ref[...], recvb_ref[...]], axis=1)
        sets = (jnp.where(core == 0, own, recv), jnp.where(core == 0, recv, own))
        blocks = []
        for s in range(2):
            w1_ref[:, CF * s : CF * s + CF] = sets[s][:, :CF]
            blocks.append(sets[s][:, CO:].astype(f32))
        wo_ref[:, :256] = sets[0][:, CF:CO]
        wo_ref[:, 256:] = sets[1][:, CF + 128 : CO]
        for p in range(pieces):
            group = []
            for c in range(2):
                for s in range(2):
                    group.append(blocks[s][unit * p : unit * p + unit, D * c : D * c + D])
            w2_ref[4 * unit * p : 4 * unit * p + 4 * unit, :] = jnp.concatenate(group, axis=0).astype(bf16)

    res = pad_rows(x_ref[0].astype(f32)) + nn(o_ref[0], wo_ref[...]) + vec[:, BO : BO + D]
    n2, r2 = norm_stats(res)
    a2 = (n2 * vec[:, G2 : G2 + D] + vec[:, B2 : B2 + D]).astype(bf16)
    a2_s[rows, :] = a2
    e = pad_rows(g_ref[0].astype(f32)) * live
    eb = e.astype(bf16)
    eb_s[rows, :] = eb
    acc = res + vec[:, BF2 : BF2 + D]
    dn = jnp.zeros((SP, D), f32)
    for c in range(FF // CH):
        cs = slice(CH * c, CH * c + CH)
        u = nn(a2, w1_ref[:, cs]) + vec[:, BF1 + CH * c : BF1 + CH * c + CH]
        dg = nt(eb, w2_ref[cs, :])
        gel, slope = gelu_parts(u)
        gb = gel.astype(bf16)
        du = (dg * slope).astype(bf16)
        gl_s[rows, cs] = gb
        du_s[rows, cs] = du
        acc = acc + nn(gb, w2_ref[cs, :])
        dn = dn + nt(du, w1_ref[:, cs])
    out_ref[0] = (acc * live)[:S]
    t = dn * vec[:, G2 : G2 + D]
    dr = e + r2 * (
        t - jnp.mean(t, axis=-1, keepdims=True) - n2 * jnp.mean(t * n2, axis=-1, keepdims=True)
    )
    dr_ref[0] = dr
    drb_s[rows, :] = dr.astype(bf16)
    sums_ref[0:1, G2 : G2 + D] += jnp.sum(dn * n2, axis=0, keepdims=True)
    sums_ref[0:1, B2 : B2 + D] += jnp.sum(dn, axis=0, keepdims=True)

    @pl.when(i == n - 1)
    def _():
        ones = jnp.ones((8, a2_s.shape[0]), bf16)
        eball = eb_s[...]
        drball = drb_s[...]
        a2t = tr(a2_s[...])
        ebt = tr(eball)
        g2 = nn(ebt, gl_s[...]).T.reshape(pieces, 4, unit, D)
        go = nn(tr(oall_ref[...].reshape(-1, D)), drball).astype(bf16)

        def put(ref, s):
            ref[:, :CF] = nn(a2t, du_s[:, CF * s : CF * s + CF]).astype(bf16)
            ref[:, CF:CO] = go[:, 128 * s : 128 * s + 256]
            for c in range(2):
                ref[:, CO + D * c : CO + D * c + D] = g2[:, 2 * c + s].reshape(D, D).astype(bf16)

        @pl.when(core == 0)
        def _():
            put(keep_ref, 0)
            put(send_ref, 1)

        @pl.when(core != 0)
        def _():
            put(keep_ref, 1)
            put(send_ref, 0)

        sums_ref[:, BF1 : BF1 + FF] = nn(ones, du_s[...])
        sums_ref[:, BF2 : BF2 + D] = nn(ones, eball)
        sums_ref[:, BO : BO + D] = nn(ones, drball)


def k2(core, counts, x, g, o, own, recv, vec, pieces, cap):
    n = x.shape[0]
    blk = lambda r, c: pl.BlockSpec((1, r, c), lambda i: (i, 0, 0))
    return pl.pallas_call(
        functools.partial(k2_kernel, pieces=pieces, cap=cap),
        name="k2",
        grid=(n,),
        in_specs=[smem(), smem(), blk(S, D), blk(S, D), blk(SP, D), full((n, SP, D)),
                  full((D, C2 // 2)), full((D, C2 // 2)), full((D, C2 // 2)), full((D, C2 // 2)), full((1, NV))],
        out_specs=[blk(S, D), blk(SP, D), full((D, C2)), full((D, C2)), full((D, D)), full((8, NV))],
        out_shape=[
            jax.ShapeDtypeStruct((n, S, D), f32),
            jax.ShapeDtypeStruct((n, SP, D), f32),
            jax.ShapeDtypeStruct((D, C2), bf16),
            jax.ShapeDtypeStruct((D, C2), bf16),
            jax.ShapeDtypeStruct((D, D), bf16),
            jax.ShapeDtypeStruct((8, NV), f32),
        ],
        scratch_shapes=[
            pltpu.VMEM((n * SP, D), bf16),
            pltpu.VMEM((n * SP, FF), bf16),
            pltpu.VMEM((n * SP, FF), bf16),
            pltpu.VMEM((n * SP, D), bf16),
            pltpu.VMEM((n * SP, D), bf16),
            pltpu.VMEM((D, FF), bf16),
            pltpu.VMEM((FF, D), bf16),
        ],
        cost_estimate=cost(n * 2e9, n * 4e6, n * 6e5),
        compiler_params=params(),
    )(core, counts, x, g, o, o, *own, *recv, vec)


def k3_kernel(qkv_ref, lse_ref, dr_ref, wo_ref, *rest):
    dp_ref = rest[-1]
    do = nt(dr_ref[0].astype(bf16), wo_ref[...]).astype(bf16)
    first = head_masks()
    lanes0 = jnp.zeros((128, SQ - SP), bf16)
    rows0 = jnp.zeros((SQ - SP, 128), bf16)
    for j in range(H // 2):
        q2 = qkv_ref[0, :, 128 * j : 128 * j + 128]
        k2_ = qkv_ref[0, :, D + 128 * j : D + 128 * j + 128]
        v2 = qkv_ref[0, :, 2 * D + 128 * j : 2 * D + 128 * j + 128]
        do2 = do[:, 128 * j : 128 * j + 128]
        q2t = jnp.concatenate([tr(q2 * 0.125), lanes0], axis=1)
        do2t = jnp.concatenate([tr(do2), lanes0], axis=1)
        k2t = tr(k2_)
        dqs = []
        dk = jnp.zeros((SP, 128), f32)
        dv = jnp.zeros((SP, 128), f32)
        for h in range(2):
            z = mask_tail(nn(pick(k2_, first, h), q2t))
            p = jnp.exp(z - lse_ref[0, pl.ds(2 * j + h, 1), :])
            dpr = nn(pick(v2, first, h), do2t)
            dot_row = jnp.sum(p * dpr, axis=0, keepdims=True)
            dz = (p * (dpr - dot_row)).astype(bf16)
            pb = p.astype(bf16)
            dv = dv + nn(pb, jnp.concatenate([pick(do2, first, h), rows0], axis=0))
            dk = dk + nn(dz, jnp.concatenate([pick(q2, first, h), rows0], axis=0))
            dqs.append(nn(k2t[HD * h : HD * h + HD, :], dz))
        dp_ref[0, :, 128 * j : 128 * j + 128] = (jnp.concatenate(dqs, axis=0).T[:SP] * 0.125).astype(bf16)
        dp_ref[0, :, D + 128 * j : D + 128 * j + 128] = (dk * 0.125).astype(bf16)
        dp_ref[0, :, 2 * D + 128 * j : 2 * D + 128 * j + 128] = dv.astype(bf16)


def k3(qkv, lse, dr, wo, start, count, prev=()):
    n = qkv.shape[0]
    blk = lambda r, c: pl.BlockSpec((1, r, c), lambda i: (i + start, 0, 0))
    return pl.pallas_call(
        k3_kernel,
        name="k3",
        grid=(count,),
        in_specs=[blk(SP, 3 * D), blk(8, SQ), blk(SP, D), full((D, D))] + [any_spec()] * len(prev),
        out_specs=blk(SP, 3 * D),
        out_shape=jax.ShapeDtypeStruct((n, SP, 3 * D), bf16),
        input_output_aliases={4 + k: k for k in range(len(prev))},
        cost_estimate=cost(count * 1.2e9, count * 2e6, count * 3e5),
        compiler_params=params(),
    )(qkv, lse, dr, wo, *prev)


def k5_kernel(x_ref, dr_ref, dp_ref, w_ref, vec_ref, dx_ref):
    dn = nt(dp_ref[0], w_ref[...])
    n1, r1 = norm_stats(x_ref[0].astype(f32))
    t = dn[:S] * vec_ref[:, G1 : G1 + D]
    dx_ref[0] = dr_ref[0, :S, :] + r1 * (
        t - jnp.mean(t, axis=-1, keepdims=True) - n1 * jnp.mean(t * n1, axis=-1, keepdims=True)
    )


def k5(x, dr, dp, w, vec):
    n = x.shape[0]
    blk = lambda r, c: pl.BlockSpec((1, r, c), lambda i: (i, 0, 0))
    return pl.pallas_call(
        k5_kernel,
        name="k5",
        grid=(n,),
        in_specs=[blk(S, D), blk(SP, D), blk(SP, 3 * D), full((D, 3 * D)), full((1, NV))],
        out_specs=blk(S, D),
        out_shape=jax.ShapeDtypeStruct((n, S, D), f32),
        cost_estimate=cost(n * 2e8, n * 2e6),
        compiler_params=params(),
    )(x, dr, dp, w, vec)


def k4_kernel(core_ref, a1_ref, n1_ref, dp_ref, w_ref, sums2_ref, keep_ref, send_ref, v_s, m_s, *, n):
    core = core_ref[0]
    dpall = dp_ref[...].reshape(-1, 3 * D)
    gq = nn(tr(a1_ref[...].reshape(-1, D)), dpall).astype(bf16)
    bsum = nn(jnp.ones((8, dpall.shape[0]), bf16), dpall)
    weight = w_ref[...].astype(f32)
    gain = jnp.sum(weight * nn(tr(n1_ref[...].reshape(-1, D)), dpall), axis=1, keepdims=True)
    shift = jnp.sum(weight * bsum[0:1, :], axis=1, keepdims=True)
    lane = lax.broadcasted_iota(jnp.int32, (D, 128), 1)
    both = jnp.where(lane == 0, gain, shift).T
    v_s[...] = sums2_ref[0:1, :]
    v_s[:, G1 : G1 + D] = both[0:1, :]
    v_s[:, B1 : B1 + D] = both[1:2, :]
    v_s[:, BQ : BQ + D] = bsum[0:1, :D]
    v_s[:, BV : BV + D] = bsum[0:1, 2 * D :]
    m_s[...] = jnp.zeros_like(m_s)
    per = D // n
    ng, nb = 2 * D // n, (NV - 2 * D) // n
    for d in range(n):
        m_s[per * d : per * d + 1, :ng] = v_s[:, ng * d : ng * d + ng]
        m_s[per * d + 1 : per * d + 2, :nb] = v_s[:, 2 * D + nb * d : 2 * D + nb * d + nb]
    small = m_s[...].astype(bf16)

    def put(ref, s):
        if s == 0:
            ref[...] = gq[:, :C1]
        else:
            ref[:, : 3 * D - C1] = gq[:, C1:]
            ref[:, 3 * D - C1 :] = small

    @pl.when(core == 0)
    def _():
        put(keep_ref, 0)
        put(send_ref, 1)

    @pl.when(core != 0)
    def _():
        put(keep_ref, 1)
        put(send_ref, 0)


def k4(core, a1, n1, dp, w, sums2, n):
    vm = pl.BlockSpec(memory_space=pltpu.VMEM)
    shape = jax.ShapeDtypeStruct((D, C1), bf16)
    return pl.pallas_call(
        functools.partial(k4_kernel, n=n), name="k4",
        in_specs=[smem()] + [vm] * 5, out_specs=[vm] * 2, out_shape=[shape] * 2,
        scratch_shapes=[pltpu.VMEM((1, NV), f32), pltpu.VMEM((D, 128), f32)],
        cost_estimate=cost(1e9, 4e6),
        compiler_params=params(),
    )(core, a1, n1, dp, w, sums2)


def last_kernel(core_ref, own1_ref, recv1_ref, own2_ref, recv2_ref, q_ref, o_ref, f1_ref, f2_ref, g_ref, b_ref):
    core = core_ref[0]
    rows = own1_ref.shape[0] // 2
    ng, nb = g_ref.shape[1], b_ref.shape[1]

    def mine(v):
        return jnp.where(core == 0, v[:rows], v[rows:])

    pairs = []
    for own_ref, recv_ref in ((own1_ref, recv1_ref), (own2_ref, recv2_ref)):
        own = own_ref[...].astype(f32)
        recv = recv_ref[...].astype(f32)
        pairs.append((jnp.where(core == 0, own, recv), jnp.where(core == 0, recv, own)))
    qkv = [mine(v) for v in pairs[0]]
    for col in range(9):
        v = qkv[0] if col < 5 else qkv[1]
        k = col if col < 5 else col - 5
        q_ref[pl.ds(col, rows, stride=9), :] = v[:, 128 * k : 128 * k + 128]
    small = qkv[1][:, 3 * D - C1 :]
    g_ref[...] = small[0:1, :ng]
    b_ref[...] = small[1:2, :nb]
    top = [mine(v[:, :CO]) for v in pairs[1]]
    for col in range(12):
        f1_ref[pl.ds(col, rows, stride=12), :] = top[col // 6][:, 128 * (col % 6) : 128 * (col % 6) + 128]
    for col in range(3):
        s, k = (0, col) if col < 2 else (1, 1)
        o_ref[pl.ds(col, rows, stride=3), :] = top[s][:, CF + 128 * k : CF + 128 * k + 128]
    for s in range(2):
        v = pairs[1][s]
        blk = jnp.where(core == 0, v[:, CO : CO + D], v[:, CO + D :])
        for col in range(3):
            f2_ref[pl.ds(3 * 2 * rows * s + col, 2 * rows, stride=3), :] = blk[:, 128 * col : 128 * col + 128]


def last(core, own1, recv1, own2, recv2):
    rows = own1.shape[0] // 2
    n = D // rows
    vm = pl.BlockSpec(memory_space=pltpu.VMEM)
    outs = [(9 * rows, 128), (3 * rows, 128), (12 * rows, 128), (12 * rows, 128), (1, 2 * D // n), (1, (NV - 2 * D) // n)]
    return pl.pallas_call(
        last_kernel, name="last", in_specs=[smem()] + [vm] * 4, out_specs=[vm] * 6,
        out_shape=[jax.ShapeDtypeStruct(s, f32) for s in outs],
        compiler_params=params(),
    )(core, own1, recv1, own2, recv2)


def swap(v, bit, n):
    return lax.ppermute(v, "fsdp", [(i, i ^ (1 << bit)) for i in range(n)])


def exchange(v, n):
    return lax.all_to_all(v, "fsdp", 0, 0, axis_index_groups=chip_groups(n))


def side(me, bit):
    return (me >> bit) & 1


def join(own, recv, axis, flag):
    low = jnp.stack([own, recv], axis)
    high = jnp.stack([recv, own], axis)
    return jnp.where(flag == 0, low, high)


def split(arr, axis, flag):
    a = lax.index_in_dim(arr, 0, axis, keepdims=False)
    b = lax.index_in_dim(arr, 1, axis, keepdims=False)
    return jnp.where(flag == 0, a, b), jnp.where(flag == 0, b, a)


def add(keep, recv):
    return (keep.astype(f32) + recv.astype(f32)).astype(bf16)


ORDERS = ((1, 2), (2, 1))


def halves_of(arr):
    cut = (arr.shape[-1] // 2) // 128 * 128
    return [arr[..., :cut], arr[..., cut:]]


def gather_chips(piece, me, n):
    top = n.bit_length() - 2
    arr = piece
    for k, bit in enumerate(range(top, 2, -1)):
        arr = join(arr, swap(arr, bit, n), k, side(me, bit))
    ax = top - 2
    chunks = halves_of(arr)
    for stage in range(2):
        got = [swap(c, o[stage], n) for c, o in zip(chunks, ORDERS)]
        chunks = [
            join(c, r, ax + 1 if (stage == 1 and o[stage] == 1) else ax, side(me, o[stage]))
            for c, r, o in zip(chunks, got, ORDERS)
        ]
    return [c.reshape(D, -1) for c in chunks]


def scatter_chips(arr, me, n):
    top = n.bit_length() - 2
    arr = arr.reshape((2,) * top + (2 * D // n, arr.shape[1]))
    chunks = halves_of(arr)
    for stage in range(2):
        pairs = [
            split(c, top - 1 if (stage == 0 and o[stage] == 1) else top - 2, side(me, o[stage]))
            for c, o in zip(chunks, ORDERS)
        ]
        got = [swap(p[1], o[stage], n) for p, o in zip(pairs, ORDERS)]
        chunks = [add(p[0], r) for p, r in zip(pairs, got)]
    arr = jnp.concatenate(chunks, axis=-1)
    for bit in range(top, 2, -1):
        keep, send = split(arr, 0, side(me, bit))
        arr = add(keep, swap(send, bit, n))
    return arr


def local_chips(n, images, counts, out_grad, qkv_weight, out_weight, fc1_weight, fc2_weight, norm_gains, biases):
    me = lax.axis_index("fsdp")
    core = (me & 1).astype(jnp.int32).reshape(1)
    chips = n // 2
    mb, cap = images.shape[:2]
    ni = mb * cap
    x = by_image(images)
    g = by_image(out_grad)
    lanes = lambda v: v.reshape(-1, 128)
    own, send = prep(core, lanes(qkv_weight), lanes(out_weight), lanes(fc1_weight), lanes(fc2_weight),
                     norm_gains.reshape(1, -1), biases.reshape(1, -1))
    p1, p2 = merge(core, own, swap(send, 0, n), chips)
    w_own = exchange(p1, n).reshape(D, C1)
    w, vec = k0(core, w_own, swap(w_own, 0, n), n)
    f_own = gather_chips(p2, me, n)
    f_recv = [swap(f, 0, n) for f in f_own]
    half = ni // 2
    saved = ()
    for part in range(2):
        saved = k1(x, w, vec, half * part, half, saved)
    a1, qkv, o, lse, n1 = saved
    out, dr, keep2, send2, wo, sums2 = k2(core, counts, x, g, o, f_own, f_recv, vec, chips, cap)
    sum2 = scatter_chips(add(keep2, swap(send2, 0, n)), me, n)
    dp = ()
    for part in range(ni):
        dp = (k3(qkv, lse, dr, wo, part, 1, dp),)
    keep1, send1 = k4(core, a1, n1, dp[0], w, sums2, n)
    sum1 = add(keep1, swap(send1, 0, n))
    sum1 = total(exchange(sum1.reshape(chips, 2 * D // n, C1), n))
    dx = k5(x, dr, dp[0], w, vec)
    grads = last(core, sum1, swap(sum1, 0, n), sum2, swap(sum2, 0, n))
    out = by_slot(out, images.shape)
    dx = by_slot(dx, images.shape)
    return (out, dx) + tuple(v.reshape(-1) for v in grads)


def by_image(v):
    mb, cap = v.shape[:2]
    tokens = lax.optimization_barrier(v.transpose(0, 2, 1, 3))
    return tokens.transpose(0, 2, 1, 3).reshape(mb * cap, S, D)


def by_slot(v, shape):
    tokens = lax.optimization_barrier(v.reshape(shape).transpose(0, 2, 1, 3))
    return tokens.transpose(0, 2, 1, 3)


def local_named(n, *args):
    return local_chips(n, *args)


def total_kernel(x_ref, o_ref):
    acc = x_ref[0].astype(f32)
    for k in range(1, x_ref.shape[0]):
        acc = acc + x_ref[k].astype(f32)
    o_ref[...] = acc.astype(bf16)


def total(x):
    vm = pl.BlockSpec(memory_space=pltpu.VMEM)
    return pl.pallas_call(
        total_kernel, name="total", in_specs=[vm], out_specs=vm,
        out_shape=jax.ShapeDtypeStruct(x.shape[1:], bf16),
        compiler_params=params(),
    )(x)


def chip_groups(n):
    return [[i for i in range(n) if i % 2 == c] for c in range(2)]


def local_any(images, counts, out_grad, qkv_weight, out_weight, fc1_weight, fc2_weight, norm_gains, biases):
    ag = lambda v: lax.all_gather(v, "fsdp", axis=0, tiled=True)
    pieces = 16
    unit = D // pieces
    zero = jnp.zeros((1,), jnp.int32)
    w = ag(qkv_weight).reshape(D, 3 * D)
    wo_in = ag(out_weight).reshape(D, D)
    w1 = ag(fc1_weight).reshape(D, FF)
    w2 = ag(fc2_weight).reshape(pieces, 2, 2, unit, D)
    vec = jnp.concatenate([ag(norm_gains), ag(biases)]).astype(f32)[None, :]
    sets = [
        jnp.concatenate([w1[:, CF * s : CF * s + CF], wo_in[:, 128 * s : 128 * s + 256],
                         w2[:, 0, s].reshape(D, D), w2[:, 1, s].reshape(D, D)], axis=1)
        for s in range(2)
    ]
    mb, cap = images.shape[:2]
    ni = mb * cap
    x = images.reshape(ni, S, D)
    g = out_grad.reshape(ni, S, D)
    a1, qkv, o, lse, n1 = k1(x, w, vec, 0, ni)
    out, dr, set0, set1, wo, sums2 = k2(zero, counts, x, g, o, halves_of(sets[0]), halves_of(sets[1]), vec, pieces, cap)
    dp = k3(qkv, lse, dr, wo, 0, ni)
    dx = k5(x, dr, dp, w, vec)
    q0, q1 = k4(zero, a1, n1, dp, w, sums2, D // 12)
    g_qkv = jnp.concatenate([q0, q1[:, : 3 * D - C1]], axis=1)
    g_out = jnp.concatenate([set0[:, CF:CO], set1[:, CF + 128 : CO]], axis=1)
    g_fc1 = jnp.concatenate([set0[:, :CF], set1[:, :CF]], axis=1)
    f2 = [jnp.stack([s[:, CO : CO + D].reshape(pieces, unit, D), s[:, CO + D :].reshape(pieces, unit, D)], 1) for s in (set0, set1)]
    g_fc2 = jnp.stack(f2, 2).reshape(FF, D)
    small = q1[:, 3 * D - C1 :].reshape(D // 12, 12, 128)
    g_gain = small[:, 0, : 2 * D * 12 // D].reshape(-1)
    g_bias = small[:, 1, : (NV - 2 * D) * 12 // D].reshape(-1)
    rs = lambda v: lax.psum_scatter(v.reshape(-1).astype(f32), "fsdp", scatter_dimension=0, tiled=True)
    return (out.reshape(images.shape), dx.reshape(images.shape)) + tuple(
        rs(v) for v in (g_qkv, g_out, g_fc1, g_fc2, g_gain, g_bias)
    )


def solution(mesh):
    n = mesh.shape["fsdp"]
    placed = (
        P(None, "fsdp", None, None),
        P(None, "fsdp"),
        P(None, "fsdp", None, None),
    ) + (P("fsdp"),) * 6
    chips = n >= 8 and n & (n - 1) == 0 and D % n == 0 and (2 * D // n) % 8 == 0
    return jax.shard_map(
        functools.partial(local_named, n) if chips else local_any,
        mesh=mesh,
        in_specs=placed,
        out_specs=(placed[0], placed[2]) + (P("fsdp"),) * 6,
        check_vma=False,
    )
```

```python
import functools
import math

import jax
import jax.numpy as jnp
from jax import lax
from jax.experimental import pallas as pl
from jax.experimental.pallas import tpu as pltpu
from jax.sharding import PartitionSpec as P


D = 384
H = 6
FF = 1536
HD = 64
S = 197
SP = 208
SQ = 256
EPS = 1e-06
f32 = jnp.float32
bf16 = jnp.bfloat16
G1, G2, B1, B2, BO, BF2, BQ, BV, BF1 = 0, 384, 768, 1152, 1536, 1920, 2304, 2688, 3072
NV = 4608
VMEM_LIMIT = 60 * 1024 * 1024


def params(**kw):
    return pltpu.CompilerParams(vmem_limit_bytes=VMEM_LIMIT, **kw)


def full(shape):
    return pl.BlockSpec(shape, lambda *_: (0,) * len(shape))


def any_spec():
    return pl.BlockSpec(memory_space=pl.ANY)


def nn(a, b):
    return jnp.dot(a, b, preferred_element_type=f32)


def nt(a, b):
    return lax.dot_general(a, b, (((1,), (1,)), ((), ())), preferred_element_type=f32)


def tr(a):
    return a.astype(f32).T.astype(a.dtype)


def norm_stats(rows):
    mean = jnp.mean(rows, axis=-1, keepdims=True)
    cen = rows - mean
    var = jnp.mean(cen * cen, axis=-1, keepdims=True)
    inv = lax.rsqrt(var + EPS)
    return cen * inv, inv


def pad_rows(ref_val):
    return jnp.concatenate([ref_val, jnp.zeros((SP - S, ref_val.shape[1]), ref_val.dtype)], axis=0)


def stack_rows(ref):
    return jnp.concatenate([pad_rows(ref[k].astype(f32)) for k in range(ref.shape[0])], axis=0)


def head_masks():
    lane = lax.broadcasted_iota(jnp.int32, (SP, 128), 1)
    return lane < HD


def pick(block, first, head):
    zero = jnp.zeros_like(block)
    return jnp.where(first, block, zero) if head == 0 else jnp.where(first, zero, block)


TAIL = S // 8 * 8
HEAD_GROUPS = (tuple(range(H)),)


def mask_tail(z):
    ok = lax.broadcasted_iota(jnp.int32, (SP - TAIL, z.shape[1]), 0) < S - TAIL
    return jnp.concatenate([z[:TAIL], jnp.where(ok, z[TAIL:], -1e30)], axis=0)


def project(x_ref, w, vec, a1_ref, qkv_ref, n1_ref):
    rows = stack_rows(x_ref)
    shape = (x_ref.shape[0], SP)
    n1, _ = norm_stats(rows)
    a1 = (n1 * vec[:, G1 : G1 + D] + vec[:, B1 : B1 + D]).astype(bf16)
    a1_ref[...] = a1.reshape(shape + (D,))
    n1_ref[...] = n1.astype(bf16).reshape(shape + (D,))
    for part, at in ((0, BQ), (1, None), (2, BV)):
        p = nn(a1, w[:, D * part : D * part + D])
        if at is not None:
            p = p + vec[:, at : at + D]
        qkv_ref[:, :, D * part : D * part + D] = p.astype(bf16).reshape(shape + (D,))


def attn_fwd_body(qkv_ref, o_ref, lse_ref):
    q = qkv_ref[0, :, :D]
    k = qkv_ref[0, :, D : 2 * D]
    v = qkv_ref[0, :, 2 * D :]
    first = head_masks()
    for group in HEAD_GROUPS:
        cols = [slice(128 * (h // 2), 128 * (h // 2) + 128) for h in group]
        q2t = [jnp.concatenate([tr(q[:, c] * 0.125), jnp.zeros((128, SQ - SP), bf16)], axis=1) for c in cols[::2]]
        v2t = [tr(v[:, c]) for c in cols[::2]]
        z = [mask_tail(nn(pick(k[:, c], first, h % 2), q2t[at // 2])) for at, (c, h) in enumerate(zip(cols, group))]
        peak = [jnp.max(s, axis=0, keepdims=True) for s in z]
        e = [jnp.exp(s - p) for s, p in zip(z, peak)]
        total = [jnp.sum(s, axis=0, keepdims=True) for s in e]
        pb = [(s * (1.0 / t)).astype(bf16) for s, t in zip(e, total)]
        outs = [nn(v2t[at // 2][HD * (at % 2) : HD * (at % 2) + HD, :], p) for at, p in enumerate(pb)]
        for at, h in enumerate(group):
            lse_ref[0, pl.ds(h, 1), :] = peak[at] + jnp.log(total[at])
        for at in range(0, len(group), 2):
            o_ref[0, :, cols[at]] = jnp.concatenate(outs[at : at + 2], axis=0).T[:SP].astype(bf16)


def cost(flops, nbytes, trans=0):
    return pl.CostEstimate(flops=int(flops), bytes_accessed=int(nbytes), transcendentals=int(trans))


def smem():
    return pl.BlockSpec(memory_space=pltpu.SMEM)


C2 = 1792
CF, CO = 768, 1024


def prep_kernel(core_ref, o_ref, f1_ref, f2_ref, own_ref, send_ref, os_, f1s, f2s):
    rows = own_ref.shape[0]
    core = core_ref[0]
    os_[...] = o_ref[...].astype(f32)
    f1s[...] = f1_ref[...].astype(f32)
    f2s[...] = f2_ref[...].astype(f32)
    sets = []
    for s in range(2):
        parts = []
        for b in range(6):
            parts.append(f1s[pl.ds(6 * s + b, rows, stride=12), :])
        for b in range(2):
            parts.append(os_[pl.ds(s + b, rows, stride=3), :])
        for half in range(2):
            for b in range(3):
                parts.append(f2s[pl.ds(3 * (2 * rows * s + rows * half) + b, rows, stride=3), :])
        sets.append(jnp.concatenate(parts, axis=1))
    own_ref[...] = jnp.where(core == 0, sets[0], sets[1]).astype(bf16)
    send_ref[...] = jnp.where(core == 0, sets[1], sets[0]).astype(bf16)


def prep(core, o, f1, f2):
    rows = o.shape[0] // 3
    shape = jax.ShapeDtypeStruct((rows, C2), bf16)
    vm = pl.BlockSpec(memory_space=pltpu.VMEM)
    return pl.pallas_call(
        prep_kernel, name="prep", in_specs=[smem()] + [vm] * 3, out_specs=[vm] * 2, out_shape=[shape] * 2,
        scratch_shapes=[pltpu.VMEM(v.shape, f32) for v in (o, f1, f2)],
        cost_estimate=cost(1e6, 2e5),
        compiler_params=params(),
    )(core, o, f1, f2)


def piece_rows(per):
    return (9 * per + 2 + 15) // 16 * 16


def piece_kernel(q_ref, g_ref, b_ref, out_ref):
    rows = q_ref.shape[0]
    wide = lambda v: jnp.concatenate([v.astype(f32), jnp.zeros((1, 128 - v.shape[1]), f32)], axis=1)
    rest = jnp.zeros((out_ref.shape[1] - rows - 2, 128), f32)
    piece = jnp.concatenate([q_ref[...].astype(f32), wide(g_ref[...]), wide(b_ref[...]), rest], axis=0).astype(bf16)
    for k in range(out_ref.shape[0]):
        out_ref[k] = piece


def piece(q, g, b, chips):
    vm = pl.BlockSpec(memory_space=pltpu.VMEM)
    return pl.pallas_call(
        piece_kernel, name="piece", in_specs=[vm] * 3, out_specs=vm,
        out_shape=jax.ShapeDtypeStruct((chips, piece_rows(q.shape[0] // 9), 128), bf16),
        compiler_params=params(),
    )(q, g, b)


def merge_kernel(core_ref, own_ref, recv_ref, p2_ref):
    core = core_ref[0]
    own = own_ref[...].astype(f32)
    recv = recv_ref[...].astype(f32)
    top = jnp.where(core == 0, own, recv)
    low = jnp.where(core == 0, recv, own)
    cat = lambda a, b: jnp.concatenate([a, b], axis=0).astype(bf16)
    p2_ref[:, :CO] = cat(top[:, :CO], low[:, :CO])
    for c, v in ((0, top), (1, low)):
        base = CO
        p2_ref[:, CO + D * c : CO + D * c + D] = cat(v[:, base : base + D], v[:, base + D : base + 2 * D])


def merge(core, own, recv):
    vm = pl.BlockSpec(memory_space=pltpu.VMEM)
    return pl.pallas_call(
        merge_kernel, name="merge", in_specs=[smem(), vm, vm], out_specs=vm,
        out_shape=jax.ShapeDtypeStruct((2 * own.shape[0], C2), bf16),
        cost_estimate=cost(1e6, 2e5),
        compiler_params=params(),
    )(core, own, recv)


def k1_kernel(qkv_ref, *rest):
    attn_fwd_body(qkv_ref, *rest[-2:])


def k1(qkv, start, count, prev=()):
    n = qkv.shape[0]
    blk = lambda r, c: pl.BlockSpec((1, r, c), lambda i: (i + start, 0, 0))
    return pl.pallas_call(
        k1_kernel,
        name="k1",
        grid=(count,),
        in_specs=[blk(SP, 3 * D)] + [any_spec()] * len(prev),
        out_specs=[blk(SP, D), blk(8, SQ)],
        out_shape=[jax.ShapeDtypeStruct((n, SP, D), bf16), jax.ShapeDtypeStruct((n, 8, SQ), f32)],
        input_output_aliases={1 + k: k for k in range(len(prev))},
        cost_estimate=cost(count * 1e9, count * 1e6, count * 3e5),
        compiler_params=params(),
    )(qkv, *prev)


def kp_kernel(core_ref, own_ref, recv_ref, x_ref, w_ref, vec_ref, a1_ref, qkv_ref, n1_ref, s_s, w_s):
    core = core_ref[0]
    s_s[core] = own_ref[...].astype(f32)
    s_s[1 - core] = recv_ref[...].astype(f32)
    chips = own_ref.shape[0]
    per = D // (2 * chips)
    ng, nb = D // chips, (NV - 2 * D) // (2 * chips)
    for d in range(2 * chips):
        for b in range(9):
            w_s[per * d : per * d + per, 128 * b : 128 * b + 128] = s_s[d % 2, d // 2, pl.ds(b, per, stride=9), :]
        vec_ref[0:1, ng * d : ng * d + ng] = s_s[d % 2, d // 2, 9 * per : 9 * per + 1, :ng]
        vec_ref[0:1, 2 * D + nb * d : 2 * D + nb * d + nb] = s_s[d % 2, d // 2, 9 * per + 1 : 9 * per + 2, :nb]
    w = w_s[...].astype(bf16)
    w_ref[...] = w
    project(x_ref, w, vec_ref[...], a1_ref, qkv_ref, n1_ref)


def kp(core, own, recv, x):
    n = x.shape[0]
    vm = pl.BlockSpec(memory_space=pltpu.VMEM)
    return pl.pallas_call(
        kp_kernel, name="kp", in_specs=[smem()] + [vm] * 3, out_specs=[vm] * 5,
        out_shape=[jax.ShapeDtypeStruct((D, 3 * D), bf16), jax.ShapeDtypeStruct((1, NV), f32)]
        + [jax.ShapeDtypeStruct((n, SP, c), bf16) for c in (D, 3 * D, D)],
        scratch_shapes=[pltpu.VMEM((2,) + own.shape, f32), pltpu.VMEM((D, 3 * D), f32)],
        cost_estimate=cost(n * 4e8, n * 2e6),
        compiler_params=params(),
    )(core, own, recv, x)


CH = 768


def gelu_parts(u):
    cum = 0.5 * (1.0 + lax.erf(u * (1.0 / math.sqrt(2.0))))
    den = jnp.exp(-0.5 * u * u) * (1.0 / math.sqrt(2.0 * math.pi))
    return u * cum, cum + u * den


def k2_kernel(core_ref, live_ref, x_ref, g_ref, o_ref, owna_ref, ownb_ref, recva_ref, recvb_ref, vec_ref,
              out_ref, dr_ref, do_ref, keep_ref, send_ref, sums_ref,
              a2_s, du_s, gl_s, eb_s, drb_s, w1_ref, w2_ref, wo_ref, *, pieces, cap):
    core = core_ref[0]
    unit = D // pieces
    vec = vec_ref[...]
    group = x_ref.shape[0]
    height = group * SP
    flags = []
    for k in range(group):
        flag = (k % cap < live_ref[k // cap]).astype(f32)
        flags.append(jnp.full((SP, 1), 1.0, f32) * flag)
    live = jnp.concatenate(flags, axis=0)

    sums_ref[...] = jnp.zeros_like(sums_ref)
    own = jnp.concatenate([owna_ref[...], ownb_ref[...]], axis=1)
    recv = jnp.concatenate([recva_ref[...], recvb_ref[...]], axis=1)
    sets = (jnp.where(core == 0, own, recv), jnp.where(core == 0, recv, own))
    blocks = []
    for s in range(2):
        w1_ref[:, CF * s : CF * s + CF] = sets[s][:, :CF]
        blocks.append(sets[s][:, CO:].astype(f32))
    wo_ref[:, :256] = sets[0][:, CF:CO]
    wo_ref[:, 256:] = sets[1][:, CF + 128 : CO]
    for p in range(pieces):
        quad = []
        for c in range(2):
            for s in range(2):
                quad.append(blocks[s][unit * p : unit * p + unit, D * c : D * c + D])
        w2_ref[4 * unit * p : 4 * unit * p + 4 * unit, :] = jnp.concatenate(quad, axis=0).astype(bf16)

    res = stack_rows(x_ref) + nn(o_ref[...].reshape(height, D), wo_ref[...]) + vec[:, BO : BO + D]
    n2, r2 = norm_stats(res)
    a2 = (n2 * vec[:, G2 : G2 + D] + vec[:, B2 : B2 + D]).astype(bf16)
    a2_s[...] = a2
    e = stack_rows(g_ref) * live
    eb = e.astype(bf16)
    eb_s[...] = eb
    acc = res + vec[:, BF2 : BF2 + D]
    dn = jnp.zeros((height, D), f32)
    for c in range(FF // CH):
        cs = slice(CH * c, CH * c + CH)
        u = nn(a2, w1_ref[:, cs]) + vec[:, BF1 + CH * c : BF1 + CH * c + CH]
        dg = nt(eb, w2_ref[cs, :])
        gel, slope = gelu_parts(u)
        gb = gel.astype(bf16)
        du = (dg * slope).astype(bf16)
        gl_s[:, cs] = gb
        du_s[:, cs] = du
        acc = acc + nn(gb, w2_ref[cs, :])
        dn = dn + nt(du, w1_ref[:, cs])
    acc = acc * live
    for k in range(group):
        out_ref[k] = acc[SP * k : SP * k + S]
    t = dn * vec[:, G2 : G2 + D]
    dr = e + r2 * (
        t - jnp.mean(t, axis=-1, keepdims=True) - n2 * jnp.mean(t * n2, axis=-1, keepdims=True)
    )
    dr_ref[...] = dr.reshape(group, SP, D)
    drb = dr.astype(bf16)
    drb_s[...] = drb
    do_ref[...] = nt(drb, wo_ref[...]).astype(bf16).reshape(group, SP, D)
    sums_ref[0:1, G2 : G2 + D] += jnp.sum(dn * n2, axis=0, keepdims=True)
    sums_ref[0:1, B2 : B2 + D] += jnp.sum(dn, axis=0, keepdims=True)

    ones = jnp.ones((8, a2_s.shape[0]), bf16)
    eball = eb_s[...]
    drball = drb_s[...]
    a2t = tr(a2_s[...])
    ebt = tr(eball)
    g2 = nn(ebt, gl_s[...]).T.reshape(pieces, 4, unit, D)
    go = nn(tr(o_ref[...].reshape(-1, D)), drball).astype(bf16)

    def put(ref, s):
        ref[:, :CF] = nn(a2t, du_s[:, CF * s : CF * s + CF]).astype(bf16)
        ref[:, CF:CO] = go[:, 128 * s : 128 * s + 256]
        for c in range(2):
            ref[:, CO + D * c : CO + D * c + D] = g2[:, 2 * c + s].reshape(D, D).astype(bf16)

    @pl.when(core == 0)
    def _():
        put(keep_ref, 0)
        put(send_ref, 1)

    @pl.when(core != 0)
    def _():
        put(keep_ref, 1)
        put(send_ref, 0)

    sums_ref[:, BF1 : BF1 + FF] = nn(ones, du_s[...])
    sums_ref[:, BF2 : BF2 + D] = nn(ones, eball)
    sums_ref[:, BO : BO + D] = nn(ones, drball)


def k2(core, counts, x, g, o, own, recv, vec, pieces, cap):
    n = x.shape[0]
    vm = pl.BlockSpec(memory_space=pltpu.VMEM)
    return pl.pallas_call(
        functools.partial(k2_kernel, pieces=pieces, cap=cap),
        name="k2",
        in_specs=[smem(), smem()] + [vm] * 8,
        out_specs=[vm] * 6,
        out_shape=[
            jax.ShapeDtypeStruct((n, S, D), f32),
            jax.ShapeDtypeStruct((n, SP, D), f32),
            jax.ShapeDtypeStruct((n, SP, D), bf16),
            jax.ShapeDtypeStruct((D, C2), bf16),
            jax.ShapeDtypeStruct((D, C2), bf16),
            jax.ShapeDtypeStruct((8, NV), f32),
        ],
        scratch_shapes=[
            pltpu.VMEM((n * SP, D), bf16),
            pltpu.VMEM((n * SP, FF), bf16),
            pltpu.VMEM((n * SP, FF), bf16),
            pltpu.VMEM((n * SP, D), bf16),
            pltpu.VMEM((n * SP, D), bf16),
            pltpu.VMEM((D, FF), bf16),
            pltpu.VMEM((FF, D), bf16),
            pltpu.VMEM((D, D), bf16),
        ],
        cost_estimate=cost(n * 2e9, n * 4e6, n * 6e5),
        compiler_params=params(),
    )(core, counts, x, g, o, *own, *recv, vec)


def k3_kernel(qkv_ref, lse_ref, do_ref, *rest):
    dp_ref = rest[-1]
    do = do_ref[0]
    first = head_masks()
    lanes0 = jnp.zeros((128, SQ - SP), bf16)
    rows0 = jnp.zeros((SQ - SP, 128), bf16)
    for group in HEAD_GROUPS:
        cols = [128 * (h // 2) for h in group[::2]]
        q2 = [qkv_ref[0, :, c : c + 128] for c in cols]
        k2_ = [qkv_ref[0, :, D + c : D + c + 128] for c in cols]
        v2 = [qkv_ref[0, :, 2 * D + c : 2 * D + c + 128] for c in cols]
        do2 = [do[:, c : c + 128] for c in cols]
        q2t = [jnp.concatenate([tr(a * 0.125), lanes0], axis=1) for a in q2]
        do2t = [jnp.concatenate([tr(a), lanes0], axis=1) for a in do2]
        k2t = [tr(a) for a in k2_]
        own = [(at // 2, h % 2, h) for at, h in enumerate(group)]
        z = [mask_tail(nn(pick(k2_[a], first, b), q2t[a])) for a, b, _ in own]
        dpr = [nn(pick(v2[a], first, b), do2t[a]) for a, b, _ in own]
        p = [jnp.exp(s - lse_ref[0, pl.ds(h, 1), :]) for s, (_, _, h) in zip(z, own)]
        dot_row = [jnp.sum(s * t, axis=0, keepdims=True) for s, t in zip(p, dpr)]
        dz = [(s * (t - r)).astype(bf16) for s, t, r in zip(p, dpr, dot_row)]
        dv = [nn(s.astype(bf16), jnp.concatenate([pick(do2[a], first, b), rows0], axis=0)) for s, (a, b, _) in zip(p, own)]
        dk = [nn(s, jnp.concatenate([pick(q2[a], first, b), rows0], axis=0)) for s, (a, b, _) in zip(dz, own)]
        dq = [nn(k2t[a][HD * b : HD * b + HD, :], s) for s, (a, b, _) in zip(dz, own)]
        for a, c in enumerate(cols):
            two = slice(2 * a, 2 * a + 2)
            dp_ref[0, :, c : c + 128] = (jnp.concatenate(dq[two], axis=0).T[:SP] * 0.125).astype(bf16)
            dp_ref[0, :, D + c : D + c + 128] = ((dk[2 * a] + dk[2 * a + 1]) * 0.125).astype(bf16)
            dp_ref[0, :, 2 * D + c : 2 * D + c + 128] = (dv[2 * a] + dv[2 * a + 1]).astype(bf16)


def k3(qkv, lse, do, start, count, prev=()):
    n = qkv.shape[0]
    blk = lambda r, c: pl.BlockSpec((1, r, c), lambda i: (i + start, 0, 0))
    return pl.pallas_call(
        k3_kernel,
        name="k3",
        grid=(count,),
        in_specs=[blk(SP, 3 * D), blk(8, SQ), blk(SP, D)] + [any_spec()] * len(prev),
        out_specs=blk(SP, 3 * D),
        out_shape=jax.ShapeDtypeStruct((n, SP, 3 * D), bf16),
        input_output_aliases={3 + k: k for k in range(len(prev))},
        cost_estimate=cost(count * 1.2e9, count * 2e6, count * 3e5),
        compiler_params=params(),
    )(qkv, lse, do, *prev)


def k5_kernel(x_ref, dr_ref, dp_ref, w_ref, vec_ref, dx_ref):
    dn = nt(dp_ref[0], w_ref[...])
    n1, r1 = norm_stats(x_ref[0].astype(f32))
    t = dn[:S] * vec_ref[:, G1 : G1 + D]
    dx_ref[0] = dr_ref[0, :S, :] + r1 * (
        t - jnp.mean(t, axis=-1, keepdims=True) - n1 * jnp.mean(t * n1, axis=-1, keepdims=True)
    )


def k5(x, dr, dp, w, vec):
    n = x.shape[0]
    blk = lambda r, c: pl.BlockSpec((1, r, c), lambda i: (i, 0, 0))
    return pl.pallas_call(
        k5_kernel,
        name="k5",
        grid=(n,),
        in_specs=[blk(S, D), blk(SP, D), blk(SP, 3 * D), full((D, 3 * D)), full((1, NV))],
        out_specs=blk(S, D),
        out_shape=jax.ShapeDtypeStruct((n, S, D), f32),
        cost_estimate=cost(n * 2e8, n * 2e6),
        compiler_params=params(),
    )(x, dr, dp, w, vec)


def k4_kernel(core_ref, a1_ref, n1_ref, dp_ref, w_ref, sums2_ref, keep_ref, send_ref, v_s, q_s, t_s):
    core = core_ref[0]
    dpall = dp_ref[...].reshape(-1, 3 * D)
    q_s[...] = nn(tr(a1_ref[...].reshape(-1, D)), dpall)
    bsum = nn(jnp.ones((8, dpall.shape[0]), bf16), dpall)
    weight = w_ref[...].astype(f32)
    gain = jnp.sum(weight * nn(tr(n1_ref[...].reshape(-1, D)), dpall), axis=1, keepdims=True)
    shift = jnp.sum(weight * bsum[0:1, :], axis=1, keepdims=True)
    lane = lax.broadcasted_iota(jnp.int32, (D, 128), 1)
    both = jnp.where(lane == 0, gain, shift).T
    v_s[...] = sums2_ref[0:1, :]
    v_s[:, G1 : G1 + D] = both[0:1, :]
    v_s[:, B1 : B1 + D] = both[1:2, :]
    v_s[:, BQ : BQ + D] = bsum[0:1, :D]
    v_s[:, BV : BV + D] = bsum[0:1, 2 * D :]
    chips = keep_ref.shape[0]
    per = D // (2 * chips)
    ng, nb = D // chips, (NV - 2 * D) // (2 * chips)
    tail = 9 * per // 8 * 8
    t_s[:, :, tail:, :] = jnp.zeros((2, chips, t_s.shape[2] - tail, 128), f32)
    for d in range(2 * chips):
        for b in range(9):
            t_s[d % 2, d // 2, pl.ds(b, per, stride=9), :] = q_s[per * d : per * d + per, 128 * b : 128 * b + 128]
        t_s[d % 2, d // 2, 9 * per : 9 * per + 1, :ng] = v_s[:, ng * d : ng * d + ng]
        t_s[d % 2, d // 2, 9 * per + 1 : 9 * per + 2, :nb] = v_s[:, 2 * D + nb * d : 2 * D + nb * d + nb]
    keep_ref[...] = t_s[core].astype(bf16)
    send_ref[...] = t_s[1 - core].astype(bf16)


def k4(core, a1, n1, dp, w, sums2, chips):
    vm = pl.BlockSpec(memory_space=pltpu.VMEM)
    rows = piece_rows(D // (2 * chips))
    shape = jax.ShapeDtypeStruct((chips, rows, 128), bf16)
    return pl.pallas_call(
        k4_kernel, name="k4",
        in_specs=[smem()] + [vm] * 5, out_specs=[vm] * 2, out_shape=[shape] * 2,
        scratch_shapes=[pltpu.VMEM((1, NV), f32), pltpu.VMEM((D, 3 * D), f32), pltpu.VMEM((2, chips, rows, 128), f32)],
        cost_estimate=cost(1e9, 4e6),
        compiler_params=params(),
    )(core, a1, n1, dp, w, sums2)


def last_kernel(core_ref, own_ref, recv_ref, o_ref, f1_ref, f2_ref):
    core = core_ref[0]
    rows = own_ref.shape[0] // 2

    def mine(v):
        return jnp.where(core == 0, v[:rows], v[rows:])

    own = own_ref[...].astype(f32)
    recv = recv_ref[...].astype(f32)
    pair = (jnp.where(core == 0, own, recv), jnp.where(core == 0, recv, own))
    top = [mine(v[:, :CO]) for v in pair]
    for col in range(12):
        f1_ref[pl.ds(col, rows, stride=12), :] = top[col // 6][:, 128 * (col % 6) : 128 * (col % 6) + 128]
    for col in range(3):
        s, k = (0, col) if col < 2 else (1, 1)
        o_ref[pl.ds(col, rows, stride=3), :] = top[s][:, CF + 128 * k : CF + 128 * k + 128]
    for s in range(2):
        v = pair[s]
        blk = jnp.where(core == 0, v[:, CO : CO + D], v[:, CO + D :])
        for col in range(3):
            f2_ref[pl.ds(3 * 2 * rows * s + col, 2 * rows, stride=3), :] = blk[:, 128 * col : 128 * col + 128]


def last(core, own, recv):
    rows = own.shape[0] // 2
    vm = pl.BlockSpec(memory_space=pltpu.VMEM)
    return pl.pallas_call(
        last_kernel, name="last", in_specs=[smem()] + [vm] * 2, out_specs=[vm] * 3,
        out_shape=[jax.ShapeDtypeStruct((k * rows, 128), f32) for k in (3, 12, 12)],
        cost_estimate=cost(1e6, 4e5),
        compiler_params=params(),
    )(core, own, recv)


def swap(v, bit, n):
    return lax.ppermute(v, "fsdp", [(i, i ^ (1 << bit)) for i in range(n)])


def exchange(v, n):
    return lax.all_to_all(v, "fsdp", 0, 0, axis_index_groups=chip_groups(n))


def side(me, bit):
    return (me >> bit) & 1


def join(own, recv, axis, flag):
    low = jnp.stack([own, recv], axis)
    high = jnp.stack([recv, own], axis)
    return jnp.where(flag == 0, low, high)


def split(arr, axis, flag):
    a = lax.index_in_dim(arr, 0, axis, keepdims=False)
    b = lax.index_in_dim(arr, 1, axis, keepdims=False)
    return jnp.where(flag == 0, a, b), jnp.where(flag == 0, b, a)


def add(keep, recv):
    return (keep.astype(f32) + recv.astype(f32)).astype(bf16)


ORDERS = ((1, 2), (2, 1))


def halves_of(arr):
    cut = (arr.shape[-1] // 2) // 128 * 128
    return [arr[..., :cut], arr[..., cut:]]


def gather_chips(piece, me, n):
    top = n.bit_length() - 2
    arr = piece
    for k, bit in enumerate(range(top, 2, -1)):
        recv = swap(arr, bit, n)
        arr = join(arr, recv, k, side(me, bit))
    ax = top - 2
    chunks = halves_of(arr)
    for stage in range(2):
        got = [swap(c, o[stage], n) for c, o in zip(chunks, ORDERS)]
        chunks = [
            join(c, r, ax + 1 if (stage == 1 and o[stage] == 1) else ax, side(me, o[stage]))
            for c, r, o in zip(chunks, got, ORDERS)
        ]
    return [c.reshape(D, -1) for c in chunks]


def scatter_chips(arr, me, n):
    top = n.bit_length() - 2
    arr = arr.reshape((2,) * top + (2 * D // n, arr.shape[1]))
    chunks = halves_of(arr)
    for stage in range(2):
        pairs = [
            split(c, top - 1 if (stage == 0 and o[stage] == 1) else top - 2, side(me, o[stage]))
            for c, o in zip(chunks, ORDERS)
        ]
        got = [swap(p[1], o[stage], n) for p, o in zip(pairs, ORDERS)]
        chunks = [add(p[0], r) for p, r in zip(pairs, got)]
    arr = jnp.concatenate(chunks, axis=-1)
    for bit in range(top, 2, -1):
        keep, send = split(arr, 0, side(me, bit))
        arr = add(keep, swap(send, bit, n))
    return arr


def local_chips(n, images, counts, out_grad, qkv_weight, out_weight, fc1_weight, fc2_weight, norm_gains, biases):
    me = lax.axis_index("fsdp")
    core = (me & 1).astype(jnp.int32).reshape(1)
    chips = n // 2
    mb, cap = images.shape[:2]
    ni = mb * cap
    x = by_image(images)
    g = by_image(out_grad)
    lanes = lambda v: v.reshape(-1, 128)
    own, send = prep(core, lanes(out_weight), lanes(fc1_weight), lanes(fc2_weight))
    first = piece(lanes(qkv_weight), norm_gains.reshape(1, -1), biases.reshape(1, -1), chips)
    q_own = exchange(first, n)
    q_recv = swap(q_own, 0, n)
    p2 = merge(core, own, swap(send, 0, n))
    f_own = gather_chips(p2, me, n)
    f_recv = [swap(f, 0, n) for f in f_own]
    w, vec, a1, qkv, n1 = kp(core, q_own, q_recv, x)
    o, lse = k1(qkv, 0, ni)
    counts = lax.optimization_barrier(counts.reshape(-1) + 0)
    out, dr, do, keep2, send2, sums2 = k2(core, counts, x, g, o, f_own, f_recv, vec, chips, cap)
    sum2 = scatter_chips(add(keep2, swap(send2, 0, n)), me, n)
    half = ni // 2
    dp = ()
    for part in range(2):
        dp = (k3(qkv, lse, do, half * part, half, dp),)
    keep1, send1 = k4(core, a1, n1, dp[0], w, sums2, chips)
    sum1 = add(keep1, swap(send1, 0, n))
    g_qkv, g_gain, g_bias = total(exchange(sum1, n))
    dx = k5(x, dr, dp[0], w, vec)
    g_out, g_fc1, g_fc2 = last(core, sum2, swap(sum2, 0, n))
    grads = (g_qkv, g_out, g_fc1, g_fc2, g_gain, g_bias)
    out = by_slot(out, images.shape)
    dx = by_slot(dx, images.shape)
    return (out, dx) + tuple(v.reshape(-1) for v in grads)


def by_image(v):
    mb, cap = v.shape[:2]
    tokens = lax.optimization_barrier(v.transpose(0, 2, 1, 3))
    return tokens.transpose(0, 2, 1, 3).reshape(mb * cap, S, D)


def by_slot(v, shape):
    tokens = lax.optimization_barrier(v.reshape(shape).transpose(0, 2, 1, 3))
    return tokens.transpose(0, 2, 1, 3)


def local_named(n, *args):
    return local_chips(n, *args)


def total_kernel(x_ref, q_ref, g_ref, b_ref):
    acc = x_ref[0].astype(f32)
    for k in range(1, x_ref.shape[0]):
        acc = acc + x_ref[k].astype(f32)
    rows = q_ref.shape[0]
    q_ref[...] = acc[:rows]
    g_ref[...] = acc[rows : rows + 1, : g_ref.shape[1]]
    b_ref[...] = acc[rows + 1 : rows + 2, : b_ref.shape[1]]


def total(x):
    vm = pl.BlockSpec(memory_space=pltpu.VMEM)
    n = 2 * x.shape[0]
    shapes = [(9 * D // n, 128), (1, 2 * D // n), (1, (NV - 2 * D) // n)]
    return pl.pallas_call(
        total_kernel, name="total", in_specs=[vm], out_specs=[vm] * 3,
        out_shape=[jax.ShapeDtypeStruct(s, f32) for s in shapes],
        compiler_params=params(),
    )(x)


def chip_groups(n):
    return [[i for i in range(n) if i % 2 == c] for c in range(2)]


def local_any(images, counts, out_grad, qkv_weight, out_weight, fc1_weight, fc2_weight, norm_gains, biases):
    ag = lambda v: lax.all_gather(v, "fsdp", axis=0, tiled=True)
    pieces = 16
    unit = D // pieces
    zero = jnp.zeros((1,), jnp.int32)
    parts = 2 * pieces
    per = D // parts
    rows = piece_rows(per)
    wide = lambda v: jnp.pad(v.reshape(parts, 1, -1), ((0, 0), (0, 0), (0, 128 - v.shape[0] // parts)))
    flat = jnp.concatenate([ag(qkv_weight).reshape(parts, 9 * per, 128), wide(ag(norm_gains)), wide(ag(biases))], axis=1)
    flat = jnp.pad(flat, ((0, 0), (0, rows - 9 * per - 2), (0, 0)))
    wo_in = ag(out_weight).reshape(D, D)
    w1 = ag(fc1_weight).reshape(D, FF)
    w2 = ag(fc2_weight).reshape(pieces, 2, 2, unit, D)
    sets = [
        jnp.concatenate([w1[:, CF * s : CF * s + CF], wo_in[:, 128 * s : 128 * s + 256],
                         w2[:, 0, s].reshape(D, D), w2[:, 1, s].reshape(D, D)], axis=1)
        for s in range(2)
    ]
    mb, cap = images.shape[:2]
    ni = mb * cap
    x = images.reshape(ni, S, D)
    g = out_grad.reshape(ni, S, D)
    w, vec, a1, qkv, n1 = kp(zero, flat[0::2], flat[1::2], x)
    o, lse = k1(qkv, 0, ni)
    out, dr, do, set0, set1, sums2 = k2(zero, counts.reshape(-1), x, g, o, halves_of(sets[0]), halves_of(sets[1]), vec, pieces, cap)
    dp = k3(qkv, lse, do, 0, ni)
    dx = k5(x, dr, dp, w, vec)
    q0, q1 = k4(zero, a1, n1, dp, w, sums2, pieces)
    q01 = jnp.stack([q0, q1], 1).reshape(parts, rows, 128)
    g_qkv = q01[:, : 9 * per]
    g_gain = q01[:, 9 * per, : 2 * D // parts]
    g_bias = q01[:, 9 * per + 1, : (NV - 2 * D) // parts]
    g_out = jnp.concatenate([set0[:, CF:CO], set1[:, CF + 128 : CO]], axis=1)
    g_fc1 = jnp.concatenate([set0[:, :CF], set1[:, :CF]], axis=1)
    f2 = [jnp.stack([s[:, CO : CO + D].reshape(pieces, unit, D), s[:, CO + D :].reshape(pieces, unit, D)], 1) for s in (set0, set1)]
    g_fc2 = jnp.stack(f2, 2).reshape(FF, D)
    rs = lambda v: lax.psum_scatter(v.reshape(-1).astype(f32), "fsdp", scatter_dimension=0, tiled=True)
    return (out.reshape(images.shape), dx.reshape(images.shape)) + tuple(
        rs(v) for v in (g_qkv, g_out, g_fc1, g_fc2, g_gain, g_bias)
    )


def solution(mesh):
    n = mesh.shape["fsdp"]
    placed = (
        P(None, "fsdp", None, None),
        P(None, "fsdp"),
        P(None, "fsdp", None, None),
    ) + (P("fsdp"),) * 6
    chips = n >= 8 and n & (n - 1) == 0 and D % n == 0 and (2 * D // n) % 8 == 0
    return jax.shard_map(
        functools.partial(local_named, n) if chips else local_any,
        mesh=mesh,
        in_specs=placed,
        out_specs=(placed[0], placed[2]) + (P("fsdp"),) * 6,
        check_vma=False,
    )
```

```python
import functools
import math

import jax
import jax.numpy as jnp
from jax import lax
from jax.experimental import pallas as pl
from jax.experimental.pallas import tpu as pltpu
from jax.sharding import PartitionSpec as P


D = 384
H = 6
FF = 1536
HD = 64
S = 197
SP = 208
SQ = 256
EPS = 1e-06
f32 = jnp.float32
bf16 = jnp.bfloat16
G1, G2, B1, B2, BO, BF2, BQ, BV, BF1 = 0, 384, 768, 1152, 1536, 1920, 2304, 2688, 3072
NV = 4608


def params(mib):
    return pltpu.CompilerParams(vmem_limit_bytes=mib * 1024 * 1024)


def full(shape):
    return pl.BlockSpec(shape, lambda *_: (0,) * len(shape))


def any_spec():
    return pl.BlockSpec(memory_space=pl.ANY)


def nn(a, b):
    return jnp.dot(a, b, preferred_element_type=f32)


def nt(a, b):
    return lax.dot_general(a, b, (((1,), (1,)), ((), ())), preferred_element_type=f32)


def tr(a):
    return a.astype(f32).T.astype(a.dtype)


def norm_stats(rows):
    mean = jnp.mean(rows, axis=-1, keepdims=True)
    cen = rows - mean
    var = jnp.mean(cen * cen, axis=-1, keepdims=True)
    inv = lax.rsqrt(var + EPS)
    return cen * inv, inv


def pad_rows(ref_val):
    return jnp.concatenate([ref_val, jnp.zeros((SP - S, ref_val.shape[1]), ref_val.dtype)], axis=0)


def stack_rows(ref):
    return jnp.concatenate([pad_rows(ref[k].astype(f32)) for k in range(ref.shape[0])], axis=0)


def head_masks():
    lane = lax.broadcasted_iota(jnp.int32, (SP, 128), 1)
    return lane < HD


def pick(block, first, head):
    zero = jnp.zeros_like(block)
    return jnp.where(first, block, zero) if head == 0 else jnp.where(first, zero, block)


TAIL = S // 8 * 8
HEAD_GROUPS = (tuple(range(H)),)


def mask_tail(z):
    ok = lax.broadcasted_iota(jnp.int32, (SP - TAIL, z.shape[1]), 0) < S - TAIL
    return jnp.concatenate([z[:TAIL], jnp.where(ok, z[TAIL:], -1e30)], axis=0)


def project(x_ref, w, vec, qkv_ref, t_ref):
    rows = stack_rows(x_ref)
    shape = (x_ref.shape[0], SP)
    n1, _ = norm_stats(rows)
    a1 = (n1 * vec[:, G1 : G1 + D] + vec[:, B1 : B1 + D]).astype(bf16)
    t_ref[:D, :] = tr(a1)
    t_ref[D:, :] = n1.T.astype(bf16)
    for part, at in ((0, BQ), (1, None), (2, BV)):
        p = nn(a1, w[:, D * part : D * part + D])
        if at is not None:
            p = p + vec[:, at : at + D]
        qkv_ref[:, :, D * part : D * part + D] = p.astype(bf16).reshape(shape + (D,))


def attn_fwd_body(qkv_ref, o_ref, lse_ref):
    q = qkv_ref[0, :, :D]
    k = qkv_ref[0, :, D : 2 * D]
    v = qkv_ref[0, :, 2 * D :]
    first = head_masks()
    for group in HEAD_GROUPS:
        cols = [slice(128 * (h // 2), 128 * (h // 2) + 128) for h in group]
        q2t = [jnp.concatenate([tr(q[:, c] * 0.125), jnp.zeros((128, SQ - SP), bf16)], axis=1) for c in cols[::2]]
        v2t = [tr(v[:, c]) for c in cols[::2]]
        z = [mask_tail(nn(pick(k[:, c], first, h % 2), q2t[at // 2])) for at, (c, h) in enumerate(zip(cols, group))]
        peak = [jnp.max(s, axis=0, keepdims=True) for s in z]
        e = [jnp.exp(s - p) for s, p in zip(z, peak)]
        total = [jnp.sum(s, axis=0, keepdims=True) for s in e]
        pb = [(s * (1.0 / t)).astype(bf16) for s, t in zip(e, total)]
        outs = [nn(v2t[at // 2][HD * (at % 2) : HD * (at % 2) + HD, :], p) for at, p in enumerate(pb)]
        for at, h in enumerate(group):
            lse_ref[0, pl.ds(h, 1), :] = peak[at] + jnp.log(total[at])
        for at in range(0, len(group), 2):
            o_ref[0, :, cols[at]] = jnp.concatenate(outs[at : at + 2], axis=0).T[:SP].astype(bf16)


def cost(flops, nbytes, trans=0):
    return pl.CostEstimate(flops=int(flops), bytes_accessed=int(nbytes), transcendentals=int(trans))


def smem():
    return pl.BlockSpec(memory_space=pltpu.SMEM)


C2 = 1792
CF, CO = 768, 1024


def prep_kernel(core_ref, o_ref, f1_ref, f2_ref, own_ref, send_ref, os_, f1s, f2s):
    rows = own_ref.shape[0]
    core = core_ref[0]
    os_[...] = o_ref[...].astype(f32)
    f1s[...] = f1_ref[...].astype(f32)
    f2s[...] = f2_ref[...].astype(f32)
    sets = []
    for s in range(2):
        parts = []
        for b in range(6):
            parts.append(f1s[pl.ds(6 * s + b, rows, stride=12), :])
        for b in range(2):
            parts.append(os_[pl.ds(s + b, rows, stride=3), :])
        for half in range(2):
            for b in range(3):
                parts.append(f2s[pl.ds(3 * (2 * rows * s + rows * half) + b, rows, stride=3), :])
        sets.append(jnp.concatenate(parts, axis=1))
    own_ref[...] = jnp.where(core == 0, sets[0], sets[1]).astype(bf16)
    send_ref[...] = jnp.where(core == 0, sets[1], sets[0]).astype(bf16)


def prep(core, o, f1, f2):
    rows = o.shape[0] // 3
    shape = jax.ShapeDtypeStruct((rows, C2), bf16)
    vm = pl.BlockSpec(memory_space=pltpu.VMEM)
    return pl.pallas_call(
        prep_kernel, name="prep", in_specs=[smem()] + [vm] * 3, out_specs=[vm] * 2, out_shape=[shape] * 2,
        scratch_shapes=[pltpu.VMEM(v.shape, f32) for v in (o, f1, f2)],
        cost_estimate=cost(1e6, 2e5),
        compiler_params=params(60),
    )(core, o, f1, f2)


def piece_rows(per):
    return (9 * per + 2 + 15) // 16 * 16


def piece_kernel(q_ref, g_ref, b_ref, out_ref):
    rows = q_ref.shape[0]
    wide = lambda v: jnp.concatenate([v.astype(f32), jnp.zeros((1, 128 - v.shape[1]), f32)], axis=1)
    rest = jnp.zeros((out_ref.shape[1] - rows - 2, 128), f32)
    piece = jnp.concatenate([q_ref[...].astype(f32), wide(g_ref[...]), wide(b_ref[...]), rest], axis=0).astype(bf16)
    for k in range(out_ref.shape[0]):
        out_ref[k] = piece


def piece(q, g, b, chips):
    vm = pl.BlockSpec(memory_space=pltpu.VMEM)
    return pl.pallas_call(
        piece_kernel, name="piece", in_specs=[vm] * 3, out_specs=vm,
        out_shape=jax.ShapeDtypeStruct((chips, piece_rows(q.shape[0] // 9), 128), bf16),
        compiler_params=params(60),
    )(q, g, b)


def merge_kernel(core_ref, own_ref, recv_ref, p2_ref):
    core = core_ref[0]
    own = own_ref[...].astype(f32)
    recv = recv_ref[...].astype(f32)
    top = jnp.where(core == 0, own, recv)
    low = jnp.where(core == 0, recv, own)
    cat = lambda a, b: jnp.concatenate([a, b], axis=0).astype(bf16)
    p2_ref[:, :CO] = cat(top[:, :CO], low[:, :CO])
    for c, v in ((0, top), (1, low)):
        base = CO
        p2_ref[:, CO + D * c : CO + D * c + D] = cat(v[:, base : base + D], v[:, base + D : base + 2 * D])


def merge(core, own, recv):
    vm = pl.BlockSpec(memory_space=pltpu.VMEM)
    return pl.pallas_call(
        merge_kernel, name="merge", in_specs=[smem(), vm, vm], out_specs=vm,
        out_shape=jax.ShapeDtypeStruct((2 * own.shape[0], C2), bf16),
        cost_estimate=cost(1e6, 2e5),
        compiler_params=params(4),
    )(core, own, recv)


def k1_kernel(qkv_ref, *rest):
    attn_fwd_body(qkv_ref, *rest[-2:])


def k1(qkv, start, count, prev=()):
    n = qkv.shape[0]
    blk = lambda r, c: pl.BlockSpec((1, r, c), lambda i: (i + start, 0, 0))
    return pl.pallas_call(
        k1_kernel,
        name="k1",
        grid=(count,),
        in_specs=[blk(SP, 3 * D)] + [any_spec()] * len(prev),
        out_specs=[blk(SP, D), blk(8, SQ)],
        out_shape=[jax.ShapeDtypeStruct((n, SP, D), bf16), jax.ShapeDtypeStruct((n, 8, SQ), f32)],
        input_output_aliases={1 + k: k for k in range(len(prev))},
        cost_estimate=cost(count * 1e9, count * 1e6, count * 3e5),
        compiler_params=params(16),
    )(qkv, *prev)


def kp_kernel(core_ref, own_ref, recv_ref, x_ref, w_ref, vec_ref, qkv_ref, t_ref, s_s, w_s):
    core = core_ref[0]
    s_s[core] = own_ref[...].astype(f32)
    s_s[1 - core] = recv_ref[...].astype(f32)
    chips = own_ref.shape[0]
    per = D // (2 * chips)
    ng, nb = D // chips, (NV - 2 * D) // (2 * chips)
    for d in range(2 * chips):
        for b in range(9):
            w_s[per * d : per * d + per, 128 * b : 128 * b + 128] = s_s[d % 2, d // 2, pl.ds(b, per, stride=9), :]
        vec_ref[0:1, ng * d : ng * d + ng] = s_s[d % 2, d // 2, 9 * per : 9 * per + 1, :ng]
        vec_ref[0:1, 2 * D + nb * d : 2 * D + nb * d + nb] = s_s[d % 2, d // 2, 9 * per + 1 : 9 * per + 2, :nb]
    w = w_s[...].astype(bf16)
    w_ref[...] = w
    project(x_ref, w, vec_ref[...], qkv_ref, t_ref)


def kp(core, own, recv, x):
    n = x.shape[0]
    vm = pl.BlockSpec(memory_space=pltpu.VMEM)
    return pl.pallas_call(
        kp_kernel, name="kp", in_specs=[smem()] + [vm] * 3, out_specs=[vm] * 4,
        out_shape=[
            jax.ShapeDtypeStruct((D, 3 * D), bf16),
            jax.ShapeDtypeStruct((1, NV), f32),
            jax.ShapeDtypeStruct((n, SP, 3 * D), bf16),
            jax.ShapeDtypeStruct((2 * D, n * SP), bf16),
        ],
        scratch_shapes=[pltpu.VMEM((2,) + own.shape, f32), pltpu.VMEM((D, 3 * D), f32)],
        cost_estimate=cost(n * 4e8, n * 2e6),
        compiler_params=params(20),
    )(core, own, recv, x)


CH = 768


def gelu_parts(u):
    cum = 0.5 * (1.0 + lax.erf(u * (1.0 / math.sqrt(2.0))))
    den = jnp.exp(-0.5 * u * u) * (1.0 / math.sqrt(2.0 * math.pi))
    return u * cum, cum + u * den


def k2_kernel(core_ref, live_ref, x_ref, g_ref, o_ref, owna_ref, ownb_ref, recva_ref, recvb_ref, vec_ref,
              out_ref, dr_ref, do_ref, keep_ref, send_ref, sums_ref,
              a2_s, du_s, gl_s, eb_s, drb_s, w1_ref, w2_ref, wo_ref, *, pieces, cap):
    core = core_ref[0]
    unit = D // pieces
    vec = vec_ref[...]
    group = x_ref.shape[0]
    height = group * SP
    flags = []
    for k in range(group):
        flag = (k % cap < live_ref[k // cap]).astype(f32)
        flags.append(jnp.full((SP, 1), 1.0, f32) * flag)
    live = jnp.concatenate(flags, axis=0)

    sums_ref[...] = jnp.zeros_like(sums_ref)
    own = jnp.concatenate([owna_ref[...], ownb_ref[...]], axis=1)
    recv = jnp.concatenate([recva_ref[...], recvb_ref[...]], axis=1)
    sets = (jnp.where(core == 0, own, recv), jnp.where(core == 0, recv, own))
    blocks = []
    for s in range(2):
        w1_ref[:, CF * s : CF * s + CF] = sets[s][:, :CF]
        blocks.append(sets[s][:, CO:].astype(f32))
    wo_ref[:, :256] = sets[0][:, CF:CO]
    wo_ref[:, 256:] = sets[1][:, CF + 128 : CO]
    for p in range(pieces):
        quad = []
        for c in range(2):
            for s in range(2):
                quad.append(blocks[s][unit * p : unit * p + unit, D * c : D * c + D])
        w2_ref[4 * unit * p : 4 * unit * p + 4 * unit, :] = jnp.concatenate(quad, axis=0).astype(bf16)

    res = stack_rows(x_ref) + nn(o_ref[...].reshape(height, D), wo_ref[...]) + vec[:, BO : BO + D]
    n2, r2 = norm_stats(res)
    a2 = (n2 * vec[:, G2 : G2 + D] + vec[:, B2 : B2 + D]).astype(bf16)
    a2_s[...] = a2
    e = stack_rows(g_ref) * live
    eb = e.astype(bf16)
    eb_s[...] = eb
    acc = res + vec[:, BF2 : BF2 + D]
    dn = jnp.zeros((height, D), f32)
    for c in range(FF // CH):
        cs = slice(CH * c, CH * c + CH)
        u = nn(a2, w1_ref[:, cs]) + vec[:, BF1 + CH * c : BF1 + CH * c + CH]
        dg = nt(eb, w2_ref[cs, :])
        gel, slope = gelu_parts(u)
        gb = gel.astype(bf16)
        du = (dg * slope).astype(bf16)
        gl_s[:, cs] = gb
        du_s[:, cs] = du
        acc = acc + nn(gb, w2_ref[cs, :])
        dn = dn + nt(du, w1_ref[:, cs])
    acc = acc * live
    for k in range(group):
        out_ref[k] = acc[SP * k : SP * k + S]
    t = dn * vec[:, G2 : G2 + D]
    dr = e + r2 * (
        t - jnp.mean(t, axis=-1, keepdims=True) - n2 * jnp.mean(t * n2, axis=-1, keepdims=True)
    )
    dr_ref[...] = dr.reshape(group, SP, D)
    drb = dr.astype(bf16)
    drb_s[...] = drb
    do_ref[...] = nt(drb, wo_ref[...]).astype(bf16).reshape(group, SP, D)
    sums_ref[0:1, G2 : G2 + D] += jnp.sum(dn * n2, axis=0, keepdims=True)
    sums_ref[0:1, B2 : B2 + D] += jnp.sum(dn, axis=0, keepdims=True)

    ones = jnp.ones((8, a2_s.shape[0]), bf16)
    eball = eb_s[...]
    drball = drb_s[...]
    a2t = tr(a2_s[...])
    ebt = tr(eball)
    g2 = nn(ebt, gl_s[...]).T.reshape(pieces, 4, unit, D)
    go = nn(tr(o_ref[...].reshape(-1, D)), drball).astype(bf16)

    def put(ref, s):
        ref[:, :CF] = nn(a2t, du_s[:, CF * s : CF * s + CF]).astype(bf16)
        ref[:, CF:CO] = go[:, 128 * s : 128 * s + 256]
        for c in range(2):
            ref[:, CO + D * c : CO + D * c + D] = g2[:, 2 * c + s].reshape(D, D).astype(bf16)

    @pl.when(core == 0)
    def _():
        put(keep_ref, 0)
        put(send_ref, 1)

    @pl.when(core != 0)
    def _():
        put(keep_ref, 1)
        put(send_ref, 0)

    sums_ref[:, BF1 : BF1 + FF] = nn(ones, du_s[...])
    sums_ref[:, BF2 : BF2 + D] = nn(ones, eball)
    sums_ref[:, BO : BO + D] = nn(ones, drball)


def k2(core, counts, x, g, o, own, recv, vec, pieces, cap):
    n = x.shape[0]
    vm = pl.BlockSpec(memory_space=pltpu.VMEM)
    return pl.pallas_call(
        functools.partial(k2_kernel, pieces=pieces, cap=cap),
        name="k2",
        in_specs=[smem(), smem()] + [vm] * 8,
        out_specs=[vm] * 6,
        out_shape=[
            jax.ShapeDtypeStruct((n, S, D), f32),
            jax.ShapeDtypeStruct((n, SP, D), f32),
            jax.ShapeDtypeStruct((n, SP, D), bf16),
            jax.ShapeDtypeStruct((D, C2), bf16),
            jax.ShapeDtypeStruct((D, C2), bf16),
            jax.ShapeDtypeStruct((8, NV), f32),
        ],
        scratch_shapes=[
            pltpu.VMEM((n * SP, D), bf16),
            pltpu.VMEM((n * SP, FF), bf16),
            pltpu.VMEM((n * SP, FF), bf16),
            pltpu.VMEM((n * SP, D), bf16),
            pltpu.VMEM((n * SP, D), bf16),
            pltpu.VMEM((D, FF), bf16),
            pltpu.VMEM((FF, D), bf16),
            pltpu.VMEM((D, D), bf16),
        ],
        cost_estimate=cost(n * 2e9, n * 4e6, n * 6e5),
        compiler_params=params(44),
    )(core, counts, x, g, o, *own, *recv, vec)


def k3_kernel(qkv_ref, lse_ref, do_ref, *rest):
    dp_ref = rest[-1]
    do = do_ref[0]
    first = head_masks()
    lanes0 = jnp.zeros((128, SQ - SP), bf16)
    rows0 = jnp.zeros((SQ - SP, 128), bf16)
    for group in HEAD_GROUPS:
        cols = [128 * (h // 2) for h in group[::2]]
        q2 = [qkv_ref[0, :, c : c + 128] for c in cols]
        k2_ = [qkv_ref[0, :, D + c : D + c + 128] for c in cols]
        v2 = [qkv_ref[0, :, 2 * D + c : 2 * D + c + 128] for c in cols]
        do2 = [do[:, c : c + 128] for c in cols]
        q2t = [jnp.concatenate([tr(a * 0.125), lanes0], axis=1) for a in q2]
        do2t = [jnp.concatenate([tr(a), lanes0], axis=1) for a in do2]
        k2t = [tr(a) for a in k2_]
        own = [(at // 2, h % 2, h) for at, h in enumerate(group)]
        z = [mask_tail(nn(pick(k2_[a], first, b), q2t[a])) for a, b, _ in own]
        dpr = [nn(pick(v2[a], first, b), do2t[a]) for a, b, _ in own]
        p = [jnp.exp(s - lse_ref[0, pl.ds(h, 1), :]) for s, (_, _, h) in zip(z, own)]
        dot_row = [jnp.sum(s * t, axis=0, keepdims=True) for s, t in zip(p, dpr)]
        dz = [(s * (t - r)).astype(bf16) for s, t, r in zip(p, dpr, dot_row)]
        dv = [nn(s.astype(bf16), jnp.concatenate([pick(do2[a], first, b), rows0], axis=0)) for s, (a, b, _) in zip(p, own)]
        dk = [nn(s, jnp.concatenate([pick(q2[a], first, b), rows0], axis=0)) for s, (a, b, _) in zip(dz, own)]
        dq = [nn(k2t[a][HD * b : HD * b + HD, :], s) for s, (a, b, _) in zip(dz, own)]
        for a, c in enumerate(cols):
            two = slice(2 * a, 2 * a + 2)
            dp_ref[0, :, c : c + 128] = (jnp.concatenate(dq[two], axis=0).T[:SP] * 0.125).astype(bf16)
            dp_ref[0, :, D + c : D + c + 128] = ((dk[2 * a] + dk[2 * a + 1]) * 0.125).astype(bf16)
            dp_ref[0, :, 2 * D + c : 2 * D + c + 128] = (dv[2 * a] + dv[2 * a + 1]).astype(bf16)


def k3(qkv, lse, do, start, count, prev=()):
    n = qkv.shape[0]
    blk = lambda r, c: pl.BlockSpec((1, r, c), lambda i: (i + start, 0, 0))
    return pl.pallas_call(
        k3_kernel,
        name="k3",
        grid=(count,),
        in_specs=[blk(SP, 3 * D), blk(8, SQ), blk(SP, D)] + [any_spec()] * len(prev),
        out_specs=blk(SP, 3 * D),
        out_shape=jax.ShapeDtypeStruct((n, SP, 3 * D), bf16),
        input_output_aliases={3 + k: k for k in range(len(prev))},
        cost_estimate=cost(count * 1.2e9, count * 2e6, count * 3e5),
        compiler_params=params(16),
    )(qkv, lse, do, *prev)


def k5_kernel(x_ref, dr_ref, dp_ref, w_ref, vec_ref, dx_ref):
    dn = nt(dp_ref[0], w_ref[...])
    n1, r1 = norm_stats(x_ref[0].astype(f32))
    t = dn[:S] * vec_ref[:, G1 : G1 + D]
    dx_ref[0] = dr_ref[0, :S, :] + r1 * (
        t - jnp.mean(t, axis=-1, keepdims=True) - n1 * jnp.mean(t * n1, axis=-1, keepdims=True)
    )


def k5(x, dr, dp, w, vec):
    n = x.shape[0]
    blk = lambda r, c: pl.BlockSpec((1, r, c), lambda i: (i, 0, 0))
    return pl.pallas_call(
        k5_kernel,
        name="k5",
        grid=(n,),
        in_specs=[blk(S, D), blk(SP, D), blk(SP, 3 * D), full((D, 3 * D)), full((1, NV))],
        out_specs=blk(S, D),
        out_shape=jax.ShapeDtypeStruct((n, S, D), f32),
        cost_estimate=cost(n * 2e8, n * 2e6),
        compiler_params=params(16),
    )(x, dr, dp, w, vec)


def k4_kernel(core_ref, rows_ref, dp_ref, w_ref, sums2_ref, keep_ref, send_ref, v_s, q_s, t_s):
    core = core_ref[0]
    dpall = dp_ref[...].reshape(-1, 3 * D)
    q_s[...] = nn(rows_ref[:D, :], dpall)
    bsum = nn(jnp.ones((8, dpall.shape[0]), bf16), dpall)
    weight = w_ref[...].astype(f32)
    gain = jnp.sum(weight * nn(rows_ref[D:, :], dpall), axis=1, keepdims=True)
    shift = jnp.sum(weight * bsum[0:1, :], axis=1, keepdims=True)
    lane = lax.broadcasted_iota(jnp.int32, (D, 128), 1)
    both = jnp.where(lane == 0, gain, shift).T
    v_s[...] = sums2_ref[0:1, :]
    v_s[:, G1 : G1 + D] = both[0:1, :]
    v_s[:, B1 : B1 + D] = both[1:2, :]
    v_s[:, BQ : BQ + D] = bsum[0:1, :D]
    v_s[:, BV : BV + D] = bsum[0:1, 2 * D :]
    chips = keep_ref.shape[0]
    per = D // (2 * chips)
    ng, nb = D // chips, (NV - 2 * D) // (2 * chips)
    tail = 9 * per // 8 * 8
    t_s[:, :, tail:, :] = jnp.zeros((2, chips, t_s.shape[2] - tail, 128), f32)
    for d in range(2 * chips):
        for b in range(9):
            t_s[d % 2, d // 2, pl.ds(b, per, stride=9), :] = q_s[per * d : per * d + per, 128 * b : 128 * b + 128]
        t_s[d % 2, d // 2, 9 * per : 9 * per + 1, :ng] = v_s[:, ng * d : ng * d + ng]
        t_s[d % 2, d // 2, 9 * per + 1 : 9 * per + 2, :nb] = v_s[:, 2 * D + nb * d : 2 * D + nb * d + nb]
    keep_ref[...] = t_s[core].astype(bf16)
    send_ref[...] = t_s[1 - core].astype(bf16)


def k4(core, rows_t, dp, w, sums2, chips):
    vm = pl.BlockSpec(memory_space=pltpu.VMEM)
    rows = piece_rows(D // (2 * chips))
    shape = jax.ShapeDtypeStruct((chips, rows, 128), bf16)
    return pl.pallas_call(
        k4_kernel, name="k4",
        in_specs=[smem()] + [vm] * 4, out_specs=[vm] * 2, out_shape=[shape] * 2,
        scratch_shapes=[pltpu.VMEM((1, NV), f32), pltpu.VMEM((D, 3 * D), f32), pltpu.VMEM((2, chips, rows, 128), f32)],
        cost_estimate=cost(1e9, 4e6),
        compiler_params=params(20),
    )(core, rows_t, dp, w, sums2)


def last_kernel(core_ref, own_ref, recv_ref, o_ref, f1_ref, f2_ref):
    core = core_ref[0]
    rows = own_ref.shape[0] // 2

    def mine(v):
        return jnp.where(core == 0, v[:rows], v[rows:])

    own = own_ref[...].astype(f32)
    recv = recv_ref[...].astype(f32)
    pair = (jnp.where(core == 0, own, recv), jnp.where(core == 0, recv, own))
    top = [mine(v[:, :CO]) for v in pair]
    for col in range(12):
        f1_ref[pl.ds(col, rows, stride=12), :] = top[col // 6][:, 128 * (col % 6) : 128 * (col % 6) + 128]
    for col in range(3):
        s, k = (0, col) if col < 2 else (1, 1)
        o_ref[pl.ds(col, rows, stride=3), :] = top[s][:, CF + 128 * k : CF + 128 * k + 128]
    for s in range(2):
        v = pair[s]
        blk = jnp.where(core == 0, v[:, CO : CO + D], v[:, CO + D :])
        for col in range(3):
            f2_ref[pl.ds(3 * 2 * rows * s + col, 2 * rows, stride=3), :] = blk[:, 128 * col : 128 * col + 128]


def last(core, own, recv):
    rows = own.shape[0] // 2
    vm = pl.BlockSpec(memory_space=pltpu.VMEM)
    return pl.pallas_call(
        last_kernel, name="last", in_specs=[smem()] + [vm] * 2, out_specs=[vm] * 3,
        out_shape=[jax.ShapeDtypeStruct((k * rows, 128), f32) for k in (3, 12, 12)],
        cost_estimate=cost(1e6, 4e5),
        compiler_params=params(4),
    )(core, own, recv)


def swap(v, bit, n):
    return lax.ppermute(v, "fsdp", [(i, i ^ (1 << bit)) for i in range(n)])


def exchange(v, n):
    return lax.all_to_all(v, "fsdp", 0, 0, axis_index_groups=chip_groups(n))


def side(me, bit):
    return (me >> bit) & 1


def join(own, recv, axis, flag):
    low = jnp.stack([own, recv], axis)
    high = jnp.stack([recv, own], axis)
    return jnp.where(flag == 0, low, high)


def split(arr, axis, flag):
    a = lax.index_in_dim(arr, 0, axis, keepdims=False)
    b = lax.index_in_dim(arr, 1, axis, keepdims=False)
    return jnp.where(flag == 0, a, b), jnp.where(flag == 0, b, a)


def add(keep, recv):
    return (keep.astype(f32) + recv.astype(f32)).astype(bf16)


ORDERS = ((1, 2), (2, 1))


def halves_of(arr):
    cut = (arr.shape[-1] // 2) // 128 * 128
    return [arr[..., :cut], arr[..., cut:]]


def gather_chips(piece, me, n):
    top = n.bit_length() - 2
    arr = piece
    for k, bit in enumerate(range(top, 2, -1)):
        recv = swap(arr, bit, n)
        arr = join(arr, recv, k, side(me, bit))
    ax = top - 2
    chunks = halves_of(arr)
    for stage in range(2):
        got = [swap(c, o[stage], n) for c, o in zip(chunks, ORDERS)]
        chunks = [
            join(c, r, ax + 1 if (stage == 1 and o[stage] == 1) else ax, side(me, o[stage]))
            for c, r, o in zip(chunks, got, ORDERS)
        ]
    return [c.reshape(D, -1) for c in chunks]


def scatter_chips(arr, me, n):
    top = n.bit_length() - 2
    arr = arr.reshape((2,) * top + (2 * D // n, arr.shape[1]))
    chunks = halves_of(arr)
    for stage in range(2):
        pairs = [
            split(c, top - 1 if (stage == 0 and o[stage] == 1) else top - 2, side(me, o[stage]))
            for c, o in zip(chunks, ORDERS)
        ]
        got = [swap(p[1], o[stage], n) for p, o in zip(pairs, ORDERS)]
        chunks = [add(p[0], r) for p, r in zip(pairs, got)]
    arr = jnp.concatenate(chunks, axis=-1)
    for bit in range(top, 2, -1):
        keep, send = split(arr, 0, side(me, bit))
        arr = add(keep, swap(send, bit, n))
    return arr


def local_chips(n, images, counts, out_grad, qkv_weight, out_weight, fc1_weight, fc2_weight, norm_gains, biases):
    me = lax.axis_index("fsdp")
    core = (me & 1).astype(jnp.int32).reshape(1)
    chips = n // 2
    mb, cap = images.shape[:2]
    ni = mb * cap
    x = by_image(images)
    g = by_image(out_grad)
    lanes = lambda v: v.reshape(-1, 128)
    own, send = prep(core, lanes(out_weight), lanes(fc1_weight), lanes(fc2_weight))
    first = piece(lanes(qkv_weight), norm_gains.reshape(1, -1), biases.reshape(1, -1), chips)
    q_own = exchange(first, n)
    q_recv = swap(q_own, 0, n)
    p2 = merge(core, own, swap(send, 0, n))
    f_own = gather_chips(p2, me, n)
    f_recv = [swap(f, 0, n) for f in f_own]
    w, vec, qkv, rows_t = kp(core, q_own, q_recv, x)
    o, lse = k1(qkv, 0, ni)
    counts = lax.optimization_barrier(counts.reshape(-1) + 0)
    out, dr, do, keep2, send2, sums2 = k2(core, counts, x, g, o, f_own, f_recv, vec, chips, cap)
    sum2 = scatter_chips(add(keep2, swap(send2, 0, n)), me, n)
    half = ni // 2
    dp = ()
    for part in range(2):
        dp = (k3(qkv, lse, do, half * part, half, dp),)
    keep1, send1 = k4(core, rows_t, dp[0], w, sums2, chips)
    sum1 = add(keep1, swap(send1, 0, n))
    g_qkv, g_gain, g_bias = total(exchange(sum1, n))
    dx = k5(x, dr, dp[0], w, vec)
    g_out, g_fc1, g_fc2 = last(core, sum2, swap(sum2, 0, n))
    grads = (g_qkv, g_out, g_fc1, g_fc2, g_gain, g_bias)
    out = by_slot(out, images.shape)
    dx = by_slot(dx, images.shape)
    return (out, dx) + tuple(v.reshape(-1) for v in grads)


def by_image(v):
    mb, cap = v.shape[:2]
    tokens = lax.optimization_barrier(v.transpose(0, 2, 1, 3))
    return tokens.transpose(0, 2, 1, 3).reshape(mb * cap, S, D)


def by_slot(v, shape):
    tokens = lax.optimization_barrier(v.reshape(shape).transpose(0, 2, 1, 3))
    return tokens.transpose(0, 2, 1, 3)


def local_named(n, *args):
    return local_chips(n, *args)


def total_kernel(x_ref, q_ref, g_ref, b_ref):
    acc = x_ref[0].astype(f32)
    for k in range(1, x_ref.shape[0]):
        acc = acc + x_ref[k].astype(f32)
    rows = q_ref.shape[0]
    q_ref[...] = acc[:rows]
    g_ref[...] = acc[rows : rows + 1, : g_ref.shape[1]]
    b_ref[...] = acc[rows + 1 : rows + 2, : b_ref.shape[1]]


def total(x):
    vm = pl.BlockSpec(memory_space=pltpu.VMEM)
    n = 2 * x.shape[0]
    shapes = [(9 * D // n, 128), (1, 2 * D // n), (1, (NV - 2 * D) // n)]
    return pl.pallas_call(
        total_kernel, name="total", in_specs=[vm], out_specs=[vm] * 3,
        out_shape=[jax.ShapeDtypeStruct(s, f32) for s in shapes],
        compiler_params=params(4),
    )(x)


def chip_groups(n):
    return [[i for i in range(n) if i % 2 == c] for c in range(2)]


def local_any(images, counts, out_grad, qkv_weight, out_weight, fc1_weight, fc2_weight, norm_gains, biases):
    ag = lambda v: lax.all_gather(v, "fsdp", axis=0, tiled=True)
    pieces = 16
    unit = D // pieces
    zero = jnp.zeros((1,), jnp.int32)
    parts = 2 * pieces
    per = D // parts
    rows = piece_rows(per)
    wide = lambda v: jnp.pad(v.reshape(parts, 1, -1), ((0, 0), (0, 0), (0, 128 - v.shape[0] // parts)))
    flat = jnp.concatenate([ag(qkv_weight).reshape(parts, 9 * per, 128), wide(ag(norm_gains)), wide(ag(biases))], axis=1)
    flat = jnp.pad(flat, ((0, 0), (0, rows - 9 * per - 2), (0, 0)))
    wo_in = ag(out_weight).reshape(D, D)
    w1 = ag(fc1_weight).reshape(D, FF)
    w2 = ag(fc2_weight).reshape(pieces, 2, 2, unit, D)
    sets = [
        jnp.concatenate([w1[:, CF * s : CF * s + CF], wo_in[:, 128 * s : 128 * s + 256],
                         w2[:, 0, s].reshape(D, D), w2[:, 1, s].reshape(D, D)], axis=1)
        for s in range(2)
    ]
    mb, cap = images.shape[:2]
    ni = mb * cap
    x = images.reshape(ni, S, D)
    g = out_grad.reshape(ni, S, D)
    w, vec, qkv, rows_t = kp(zero, flat[0::2], flat[1::2], x)
    o, lse = k1(qkv, 0, ni)
    out, dr, do, set0, set1, sums2 = k2(zero, counts.reshape(-1), x, g, o, halves_of(sets[0]), halves_of(sets[1]), vec, pieces, cap)
    dp = k3(qkv, lse, do, 0, ni)
    dx = k5(x, dr, dp, w, vec)
    q0, q1 = k4(zero, rows_t, dp, w, sums2, pieces)
    q01 = jnp.stack([q0, q1], 1).reshape(parts, rows, 128)
    g_qkv = q01[:, : 9 * per]
    g_gain = q01[:, 9 * per, : 2 * D // parts]
    g_bias = q01[:, 9 * per + 1, : (NV - 2 * D) // parts]
    g_out = jnp.concatenate([set0[:, CF:CO], set1[:, CF + 128 : CO]], axis=1)
    g_fc1 = jnp.concatenate([set0[:, :CF], set1[:, :CF]], axis=1)
    f2 = [jnp.stack([s[:, CO : CO + D].reshape(pieces, unit, D), s[:, CO + D :].reshape(pieces, unit, D)], 1) for s in (set0, set1)]
    g_fc2 = jnp.stack(f2, 2).reshape(FF, D)
    rs = lambda v: lax.psum_scatter(v.reshape(-1).astype(f32), "fsdp", scatter_dimension=0, tiled=True)
    return (out.reshape(images.shape), dx.reshape(images.shape)) + tuple(
        rs(v) for v in (g_qkv, g_out, g_fc1, g_fc2, g_gain, g_bias)
    )


def solution(mesh):
    n = mesh.shape["fsdp"]
    placed = (
        P(None, "fsdp", None, None),
        P(None, "fsdp"),
        P(None, "fsdp", None, None),
    ) + (P("fsdp"),) * 6
    chips = n >= 8 and n & (n - 1) == 0 and D % n == 0 and (2 * D // n) % 8 == 0
    return jax.shard_map(
        functools.partial(local_named, n) if chips else local_any,
        mesh=mesh,
        in_specs=placed,
        out_specs=(placed[0], placed[2]) + (P("fsdp"),) * 6,
        check_vma=False,
    )
```
